32 devices in a mesh: net: 2 (over y), obs: 4 (over z), state: 4 (over x, core).
Axes of the slice: x: 2, y: 2, z: 4, core: 2. Of those that a mesh axis runs over, the one named last changes fastest.
Arguments:
- anomalies: bfloat16 [4, 512, 512], P('state', 'obs'), may hold values from -6 to 6
- prior_ensemble_mean: float32 [4, 512], P('state', 'obs'), may hold values from -6 to 6
- operator_blocks: bfloat16 [64, 4, 8, 128, 128], P(('net', 'obs'), 'state'), parts along dimension 0, may hold values from -0.09375 to 0.09375
- block_column_ids: int32 [64, 4, 8], P(('net', 'obs'), 'state'), parts along dimension 0, may hold values from 0 to 3
- observation_counts: int32 [64], P(('net', 'obs')), parts along dimension 0, may hold values from 1 to 128, as said below
- observed_readings: float32 [64, 128], P(('net', 'obs')), parts along dimension 0, may hold values from -6 to 6
- observation_error_std: float32 [64, 128], P(('net', 'obs')), parts along dimension 0, may hold values from 0.25 to 4
Outputs:
- analysis: bfloat16 [8, 512, 512], P(('net', 'state'), 'obs'), parts along dimension 0
The draws below stay inside these ranges and needn't reach their ends.
There are 2 independent parts, one for each index of `net`. The reference program is written for one: setup_inputs(seed, part) draws one part's arguments, and reference() takes and returns one part's arrays. A program takes and returns all parts, laid end to end along the dimension named above; an argument that names none is the same for every part. Nothing has to cross between parts.
Inputs may be any that keep to these rules, and one draw needn't show every extreme that they name: `observation_counts`: some observation block of every network is full.
All inputs are finite; a program needn't handle non-finite values.
Results may differ from the reference program's by a relative error of at most 0.0053.
Values may be sent and summed in bfloat16 or wider, within the bound.
A program may use at most 64 MiB of HBM per device.

```python
import math
import jax
import jax.numpy as jnp
from jax import lax

MEMBERS = 512
BLOCK_SIZE = 128
NB = 8
STATE_SLAB_COUNT = 4
SLAB_CELL_COUNT = 512
SLAB_BLOCK_COUNT = 4
OBLKS = 32


def draw_observation_counts(key, part):
    first, second = jax.random.split(jax.random.fold_in(key, 11))
    counts = jax.random.randint(first, (OBLKS,), 1, BLOCK_SIZE + 1)
    full_at = jax.random.randint(second, (), 0, OBLKS)
    return jnp.where(jnp.arange(OBLKS) == full_at, BLOCK_SIZE, counts).astype(jnp.int32)


def set_ends(drawn, own_key, smallest, high):
    index_at = [jax.random.randint(jax.random.fold_in(own_key, axis), (), 0, length) for axis, length in enumerate(drawn.shape)]
    longest = drawn.shape.index(max(drawn.shape))
    next_to = index_at[:longest] + [(index_at[longest] + 1) % drawn.shape[longest]] + index_at[longest + 1:]
    return drawn.at[tuple(index_at)].set(smallest).at[tuple(next_to)].set(high)


def level_of(stream_key, shape, cuts, smallest, top_value):
    loudness, own = 1.0, jax.random.fold_in(stream_key, 6)
    for axis_at, parts in cuts:
        heights = jnp.exp(jax.random.uniform(jax.random.fold_in(own, axis_at), (parts,), jnp.float32, smallest / len(cuts), top_value / len(cuts)))
        loudness = loudness * jnp.repeat(heights, shape[axis_at] // parts).reshape([-1 if axis == axis_at else 1 for axis in range(len(shape))])
    return loudness


def bell_draw(key, shape, width, limit, pieces=(), kind=jnp.bfloat16):
    entries = jax.random.normal(key, shape, jnp.float32) * width
    if len(pieces) > 0:
        entries = level_of(key, shape, pieces, -0.22, 0.18) * entries
    return jnp.clip(entries, min=-limit, max=limit).astype(kind)


def setup_inputs(seed: int = 0, part: int = 0) -> dict:
    key_list = jax.random.split(jax.random.key(seed), 8)
    part_keys = jax.random.split(jax.random.fold_in(key_list[7], part), 8)
    anomalies = bell_draw(key_list[0], (STATE_SLAB_COUNT, SLAB_CELL_COUNT, MEMBERS), 1.0, 6.0, ((0, 4), (1, 4)))
    prior_ensemble_mean = bell_draw(key_list[1], (STATE_SLAB_COUNT, SLAB_CELL_COUNT), 1.0, 6.0, ((0, 4), (1, 4)), jnp.float32)
    operator_blocks = bell_draw(part_keys[2], (OBLKS, STATE_SLAB_COUNT, NB, BLOCK_SIZE, BLOCK_SIZE), (STATE_SLAB_COUNT * NB * BLOCK_SIZE) ** -0.5, 0.09375, ((0, 4), (1, 4)))
    block_column_ids = set_ends(jax.random.randint(part_keys[3], (OBLKS, STATE_SLAB_COUNT, NB), 0, SLAB_BLOCK_COUNT), jax.random.fold_in(part_keys[3], 1), 0, SLAB_BLOCK_COUNT - 1).astype(jnp.int32)
    observation_counts = draw_observation_counts(jax.random.fold_in(jax.random.fold_in(key_list[7], part), 71), part)
    observed_readings = jnp.clip(jax.random.uniform(part_keys[5], (OBLKS, BLOCK_SIZE), jnp.float32, -6.0, 6.0) * level_of(part_keys[5], (OBLKS, BLOCK_SIZE), ((0, 4),), -0.4, 0.0), -6.0, 6.0)
    observation_error_std = jnp.clip(jnp.exp(math.log(4.0) - 2.7725887 * jax.random.uniform(part_keys[6], (OBLKS, BLOCK_SIZE), jnp.float32) ** level_of(part_keys[6], (OBLKS, BLOCK_SIZE), ((0, 4),), -0.2, 0.2)), 0.25, 4.0)
    return dict(anomalies=anomalies, prior_ensemble_mean=prior_ensemble_mean, operator_blocks=operator_blocks, block_column_ids=block_column_ids, observation_counts=observation_counts, observed_readings=observed_readings, observation_error_std=observation_error_std)


def reference(anomalies, prior_ensemble_mean, operator_blocks, block_column_ids, observation_counts, observed_readings, observation_error_std):
    members = anomalies.shape[2]
    cells = anomalies.reshape(STATE_SLAB_COUNT, SLAB_BLOCK_COUNT, BLOCK_SIZE, members)
    reduced_mean = prior_ensemble_mean.astype(jnp.bfloat16).reshape(STATE_SLAB_COUNT, SLAB_BLOCK_COUNT, BLOCK_SIZE)
    slab_ids = jnp.arange(STATE_SLAB_COUNT, dtype=jnp.int32)[:, None]

    def one_block(inputs):
        values, columns = inputs
        picked = cells[slab_ids, columns]
        picked_mean = reduced_mean[slab_ids, columns]
        wide = values.astype(jnp.float32)
        rows_anom = jnp.einsum('sjrc,sjck->rk', wide, picked.astype(jnp.float32))
        rows_mean = jnp.einsum('sjrc,sjc->r', wide, picked_mean.astype(jnp.float32))
        return (rows_anom, rows_mean)
    obs_anom, obs_mean = lax.map(one_block, (operator_blocks, block_column_ids))
    obs_anom = obs_anom.reshape(OBLKS * BLOCK_SIZE, members)
    obs_mean = obs_mean.reshape(OBLKS * BLOCK_SIZE)
    valid = (jnp.arange(BLOCK_SIZE, dtype=jnp.int32)[None, :] < observation_counts[:, None]).astype(jnp.float32)
    weight = (valid / observation_error_std).reshape(OBLKS * BLOCK_SIZE)
    scaled = obs_anom * weight[:, None]
    innovation = weight * (observed_readings.reshape(OBLKS * BLOCK_SIZE) - obs_mean)
    gram = jnp.dot(scaled.T, scaled, precision=lax.Precision.HIGHEST)
    gram = gram + (members - 1.0) * jnp.eye(members, dtype=jnp.float32)
    rhs = jnp.dot(scaled.T, innovation[:, None], precision=lax.Precision.HIGHEST)
    lower = jnp.linalg.cholesky(gram)
    middle = lax.linalg.triangular_solve(lower, rhs, left_side=True, lower=True)
    mean_weights = lax.linalg.triangular_solve(lower, middle, left_side=True, lower=True, transpose_a=True)
    identity = jnp.eye(members, dtype=jnp.float32)
    transform = jnp.sqrt(members - 1.0) * lax.linalg.triangular_solve(lower, identity, left_side=True, lower=True, transpose_a=True)
    mixing = (transform + mean_weights).astype(jnp.bfloat16)
    flat = anomalies.reshape(STATE_SLAB_COUNT * SLAB_CELL_COUNT, members)
    shifted_values = jnp.dot(flat.astype(jnp.float32), mixing.astype(jnp.float32), preferred_element_type=jnp.float32)
    analysis_output = prior_ensemble_mean.reshape(STATE_SLAB_COUNT * SLAB_CELL_COUNT)[:, None] + shifted_values
    return analysis_output.astype(jnp.bfloat16).reshape(STATE_SLAB_COUNT, SLAB_CELL_COUNT, members)
```

```python
import functools
import jax
import jax.numpy as jnp
from jax import lax
from jax.experimental import pallas as pl
from jax.experimental.pallas import tpu as pltpu
from jax.sharding import PartitionSpec as P

BLK = 128
HI = lax.Precision.HIGHEST
NT = (((1,), (1,)), ((), ()))


TN = (((0,), (0,)), ((), ()))


def split(x):
    high = x.astype(jnp.bfloat16)
    return high, (x - high.astype(jnp.float32)).astype(jnp.bfloat16)


def joined(x, y, axis, dims):
    (xh, xl), (yh, yl) = x, y
    return lax.dot_general(
        jnp.concatenate([xh, xh, xl], axis=axis), jnp.concatenate([yh, yl, yh], axis=axis), dims,
        preferred_element_type=jnp.float32,
    )


def times_transposed(x, y):
    return joined(x, y, 1, NT)


def transposed_times(x, y):
    return joined(x, y, 0, TN)


def inverse_factor(block, width=32):
    row = lax.broadcasted_iota(jnp.int32, (BLK, BLK), 0)
    col = lax.broadcasted_iota(jnp.int32, (BLK, BLK), 1)
    eye = (row == col).astype(jnp.float32)
    groups = BLK // 8
    left = [block[8 * g : 8 * g + 8] for g in range(groups)]
    right = [eye[8 * g : 8 * g + 8] for g in range(groups)]
    sub = lax.broadcasted_iota(jnp.int32, (8, 1), 0)
    lane = lax.broadcasted_iota(jnp.int32, (1, BLK), 1)
    local = width // 8
    for start in range(0, BLK, width):
        g0 = start // 8
        spread = [
            [
                None if h < j // 8
                else jnp.broadcast_to(left[g0 + h][:, start + j : start + j + 1], (8, BLK))
                for h in range(local)
            ]
            for j in range(width)
        ]
        scaled = []
        roots = []
        for j in range(width):
            gj, ij = divmod(j, 8)
            pivot = spread[j][gj][ij : ij + 1]
            inv = 1.0 / pivot
            roots.append(lax.rsqrt(pivot))
            lrow = left[g0 + gj][ij : ij + 1]
            rrow = right[g0 + gj][ij : ij + 1]
            scaled.append(lrow * inv)
            ms = {}
            for h in range(gj, local):
                m = spread[j][h]
                if h == gj:
                    if ij == 7:
                        continue
                    m = jnp.where(sub > ij, m, 0.0)
                ms[h] = m * inv
            for t in range(j + 1, width):
                gt, it = divmod(t, 8)
                shared = spread[j][gt][it : it + 1]
                for h in range(gt, local):
                    if h in ms:
                        spread[t][h] = spread[t][h] - ms[h] * shared
            for h in ms:
                left[g0 + h] = left[g0 + h] - ms[h] * lrow
                right[g0 + h] = right[g0 + h] - ms[h] * rrow
        upper_l = jnp.concatenate(left[g0 : g0 + local], axis=0)
        upper_r = jnp.concatenate(right[g0 : g0 + local], axis=0)
        end = start + width
        if end < BLK:
            low = jnp.where(lane >= end, jnp.concatenate(scaled, axis=0), 0.0)
            change = transposed_times(
                split(low), split(jnp.concatenate([upper_l, upper_r], axis=1))
            )
            for h in range(end // 8, groups):
                left[h] = left[h] - change[8 * h : 8 * h + 8, :BLK]
                right[h] = right[h] - change[8 * h : 8 * h + 8, BLK:]
        scale = jnp.concatenate(roots, axis=0)
        for h in range(local):
            right[g0 + h] = right[g0 + h] * scale[8 * h : 8 * h + 8]
    return jnp.concatenate(right, axis=0)


def finish_kernel(packed_ref, anom_ref, mean_ref, out_ref, work):
    cells, members = anom_ref.shape
    total = members + cells + 8
    row = lax.broadcasted_iota(jnp.int32, (BLK, BLK), 0)
    col = lax.broadcasted_iota(jnp.int32, (BLK, BLK), 1)
    ridge = jnp.where(row == col, members - 1.0, 0.0)
    start = 0
    last = packed_ref.shape[0] - 8
    for j in range(members // BLK):
        size = members - j * BLK
        cols = slice(j * BLK, (j + 1) * BLK)
        if j:
            work[0 : j * BLK, cols] = jnp.zeros((j * BLK, BLK), jnp.float32)
        work[cols, cols] = packed_ref[start : start + BLK, :] + ridge
        if size > BLK:
            work[(j + 1) * BLK : members, cols] = packed_ref[start + BLK : start + size, :]
        start += size
    for j in range(members // BLK):
        cols = slice(j * BLK, (j + 1) * BLK)
        work[members + cells : total, cols] = jnp.broadcast_to(
            packed_ref[last + j : last + j + 1, :], (8, BLK)
        )
    work[members : members + cells, :] = anom_ref[...].astype(jnp.float32)

    for off in range(0, members, BLK):
        end = off + BLK
        inv = inverse_factor(work[off:end, off:end])
        x = lax.dot_general(
            work[end:total, off:end], inv, NT, precision=HI, preferred_element_type=jnp.float32
        )
        work[members:total, off:end] = x[members - end :]
        if end < members:
            work[end : end + BLK, end : end + BLK] -= lax.dot_general(
                x[:BLK], x[:BLK], NT, precision=HI, preferred_element_type=jnp.float32
            )
            work[end + BLK : total, end : end + BLK] -= lax.dot_general(
                x[BLK:], x[:BLK], NT, precision=HI, preferred_element_type=jnp.float32
            )
        for at in range(end + BLK, members, BLK):
            work[at:total, at : at + BLK] -= lax.dot_general(
                x[at - end :], x[at - end : at - end + BLK], NT, precision=HI,
                preferred_element_type=jnp.float32,
            )

    solved = work[members : members + cells, :]
    shift = jnp.sum(solved * work[members + cells : members + cells + 1, :], axis=1, keepdims=True)
    root = (members - 1.0) ** 0.5
    mean = jnp.broadcast_to(mean_ref[...], (BLK, cells)).T[:, 0:1]
    out_ref[...] = (mean + (root * solved + shift)).astype(jnp.bfloat16)


def finish(packed, cells, mean_row):
    ncells, members = cells.shape
    return pl.pallas_call(
        finish_kernel,
        out_shape=jax.ShapeDtypeStruct((ncells, members), jnp.bfloat16),
        in_specs=[pl.BlockSpec(memory_space=pltpu.VMEM)] * 3,
        out_specs=pl.BlockSpec(memory_space=pltpu.VMEM),
        scratch_shapes=[pltpu.VMEM((members + ncells + 8, members), jnp.float32)],
        compiler_params=pltpu.CompilerParams(vmem_limit_bytes=32 << 20),
    )(packed, cells, mean_row)


def packed_rows(members, ways):
    need = sum(members - j * BLK for j in range(members // BLK))
    step = 16 * ways
    return (need + step - 1) // step * step


def bits_of(n):
    return [1 << t for t in range(n.bit_length() - 1)]


def observe_kernel(
    obs_n, state_n, ids_ref, counts_ref, cells_hbm, mean_hbm, ops_hbm, read_hbm, std_hbm, out_ref,
    mean_row, ops_ref, read_ref, std_ref, load_sem,
    slab, slab_mean, part, sent, got, inno, inno_got, acc, acc_got, full, rhs_sum, rhs_got,
    right_send, right_recv, left_send, left_recv, part_send, part_recv, inno_send, inno_recv,
    acc_send, acc_recv, rhs_send, rhs_recv,
):
    me_o, me_s = lax.axis_index("obs"), lax.axis_index("state")
    nb, slots = ops_ref.shape[0], ops_ref.shape[1]
    members = slab.shape[2]
    state_bits, obs_bits = bits_of(state_n), bits_of(obs_n)

    loads = [
        pltpu.make_async_copy(src, dst, load_sem.at[n])
        for n, (src, dst) in enumerate([
            (cells_hbm, slab.at[me_o]), (mean_hbm, mean_row), (read_hbm, read_ref),
            (std_hbm, std_ref), (ops_hbm, ops_ref),
        ])
    ]
    for load in loads:
        load.start()

    def partner(axis, bit):
        me = me_s if axis == "state" else me_o
        return me + bit - 2 * bit * ((me // bit) % 2)

    barrier = pltpu.get_barrier_semaphore()
    greeted = [{"obs": lax.rem(me_o + 1, obs_n)}, {"obs": lax.rem(me_o + obs_n - 1, obs_n)}]
    greeted += [{"obs": partner("obs", b)} for b in obs_bits]
    greeted += [{"state": partner("state", b)} for b in state_bits]
    for where in greeted:
        pl.semaphore_signal(barrier, inc=1, device_id=where, device_id_type=pl.DeviceIdType.MESH)
    loads[0].wait()
    loads[1].wait()
    slab_mean[me_o] = jnp.broadcast_to(mean_row[...], (16, BLK)).astype(jnp.bfloat16)
    pl.semaphore_wait(barrier, len(greeted))

    def remote(src, dst, send, recv, where):
        return pltpu.make_async_remote_copy(
            src_ref=src, dst_ref=dst, send_sem=send, recv_sem=recv,
            device_id=where, device_id_type=pl.DeviceIdType.MESH,
        )

    def hop(block, sends, recvs, t, to):
        return [
            remote(slab.at[block], slab.at[block], sends.at[0, t], recvs.at[0, t], {"obs": to}),
            remote(slab_mean.at[block], slab_mean.at[block], sends.at[1, t], recvs.at[1, t], {"obs": to}),
        ]

    def clip(x):
        return jnp.clip(x, 0, obs_n - 1)

    for t in range(obs_n - 1):
        @pl.when((me_o < obs_n - 1) & (me_o - t >= 0))
        def _():
            for c in hop(clip(me_o - t), right_send, right_recv, t, clip(me_o + 1)):
                c.start()

        @pl.when((me_o > 0) & (me_o + t <= obs_n - 1))
        def _():
            for c in hop(clip(me_o + t), left_send, left_recv, t, clip(me_o - 1)):
                c.start()

        @pl.when(me_o - 1 - t >= 0)
        def _():
            for c in hop(clip(me_o - 1 - t), right_send, right_recv, t, clip(me_o - 1)):
                c.wait_recv()

        @pl.when(me_o + 1 + t <= obs_n - 1)
        def _():
            for c in hop(clip(me_o + 1 + t), left_send, left_recv, t, clip(me_o + 1)):
                c.wait_recv()

    for load in loads[2:]:
        load.wait()
    lane = lax.broadcasted_iota(jnp.int32, (1, BLK), 1)

    def weight_of(b):
        return jnp.where(lane < counts_ref[b], 1.0 / std_ref[pl.ds(b, 1), :], 0.0)

    @pl.loop(0, nb)
    def _(b):
        mean = jnp.zeros((16, BLK), jnp.float32)
        for j in range(slots):
            mean += lax.dot_general(
                slab_mean[ids_ref[b, j]], ops_ref[b, j], NT, preferred_element_type=jnp.float32
            )
        share = read_ref[pl.ds(b, 1), :] * (1.0 / state_n)
        inno[pl.ds(b, 1), :] = weight_of(b) * (share - mean[0:1])

    def inno_copy(t):
        where = {"state": partner("state", state_bits[t])}
        return remote(inno, inno_got.at[t], inno_send.at[t], inno_recv.at[t], where)

    inno_copy(0).start()

    def observe(b):
        rows = jnp.zeros((BLK, members), jnp.float32)
        for j in range(slots):
            rows += jnp.dot(ops_ref[b, j], slab[ids_ref[b, j]], preferred_element_type=jnp.float32)
        return rows * jnp.broadcast_to(weight_of(b), (BLK, BLK)).T[:, 0:1]

    def part_copy(t, i):
        n = nb - (nb >> t) + i
        where = {"state": partner("state", state_bits[t])}
        return remote(sent.at[n], got.at[n], part_send.at[n], part_recv.at[n], where)

    lows = [0]
    for t, bit in enumerate(state_bits):
        half = nb >> (t + 1)
        keep = (me_s // bit) % 2 * half
        give = lows[-1] + half - keep
        lows.append(lows[-1] + keep)

        def total(b, upto):
            value = observe(b)
            for u in range(upto):
                part_copy(u, b - lows[u + 1]).wait_recv()
                value += got[nb - (nb >> u) + b - lows[u + 1]].astype(jnp.float32)
            return value

        @pl.loop(0, half)
        def _(i):
            sent[nb - (nb >> t) + i] = total(give + i, t).astype(jnp.bfloat16)
            part_copy(t, i).start()

        inno_copy(t).wait()
        inno[...] += inno_got[t]
        if t + 1 < len(state_bits):
            inno_copy(t + 1).start()
    own = nb // state_n
    low = lows[-1]
    last = len(state_bits) - 1

    @pl.loop(0, own)
    def _(i):
        value = observe(low + i)
        for u in range(last):
            part_copy(u, low + i - lows[u + 1]).wait_recv()
            value += got[nb - (nb >> u) + low + i - lows[u + 1]].astype(jnp.float32)
        part[i] = value

    @pl.loop(0, own)
    def _(i):
        part_copy(last, i).wait_recv()
        part[i] += got[nb - (nb >> last) + i].astype(jnp.float32)

    scaled = part[...].reshape(own * BLK, members)
    row = 0
    for j in range(members // BLK):
        size = members - j * BLK
        acc[row : row + size, :] = lax.dot_general(
            scaled[:, j * BLK :], scaled[:, j * BLK : (j + 1) * BLK], (((0,), (0,)), ((), ())),
            precision=HI, preferred_element_type=jnp.float32,
        )
        row += size
    if row < acc.shape[0]:
        acc[row:, :] = jnp.zeros((acc.shape[0] - row, BLK), jnp.float32)
    rhs = jnp.zeros((8, members), jnp.float32)
    for i in range(own):
        rhs += jnp.dot(
            jnp.broadcast_to(inno[pl.ds(low + i, 1), :], (8, BLK)), scaled[i * BLK : (i + 1) * BLK],
            precision=HI, preferred_element_type=jnp.float32,
        )
    rhs_sum[...] = jnp.zeros((8, BLK), jnp.float32)
    for j in range(members // BLK):
        rhs_sum[j : j + 1, :] = rhs[0:1, j * BLK : (j + 1) * BLK]

    by_state = [("state", b) for b in state_bits]
    by_obs = [("obs", b) for b in obs_bits]
    orders = [by_state + by_obs, by_state[:1] + by_obs + by_state[1:]]
    steps = len(orders[0])
    size = acc.shape[0] // 2
    bases = [0, size]
    spots = [0, size]
    trail = []
    for n in range(steps):
        size //= 2
        copies = []
        for k in range(2):
            axis, bit = orders[k][n]
            keep = ((me_s if axis == "state" else me_o) // bit) % 2 * size
            where = {axis: partner(axis, bit)}
            give = pl.multiple_of(bases[k] + size - keep, 8)
            copies.append(remote(
                acc.at[pl.ds(give, size)], acc_got.at[pl.ds(spots[k], size)],
                acc_send.at[k, n], acc_recv.at[k, n], where,
            ))
            bases[k] = pl.multiple_of(bases[k] + keep, 8)
            trail.append((k, n, where, bases[k], size))
            if k == 0:
                copies.append(remote(rhs_sum, rhs_got.at[n], rhs_send.at[n], rhs_recv.at[n], where))
        for copy in copies:
            copy.start()
        for copy in copies:
            copy.wait()
        for k in range(2):
            acc[pl.ds(bases[k], size), :] += acc_got[spots[k] : spots[k] + size, :]
            spots[k] += size
        rhs_sum[...] += rhs_got[n]
    for k in range(2):
        full[pl.ds(bases[k], size), :] = acc[pl.ds(bases[k], size), :]
    for n in reversed(range(steps)):
        copies = [
            remote(
                full.at[pl.ds(base, size)], full.at[pl.ds(base, size)],
                acc_send.at[k, steps + n], acc_recv.at[k, steps + n], where,
            )
            for k, m, where, base, size in trail if m == n
        ]
        for copy in copies:
            copy.start()
        for copy in copies:
            copy.wait()

    for t in range(obs_n - 1):
        @pl.when((me_o < obs_n - 1) & (me_o - t >= 0))
        def _():
            for c in hop(clip(me_o - t), right_send, right_recv, t, clip(me_o + 1)):
                c.wait_send()

        @pl.when((me_o > 0) & (me_o + t <= obs_n - 1))
        def _():
            for c in hop(clip(me_o + t), left_send, left_recv, t, clip(me_o - 1)):
                c.wait_send()
    for t in range(len(state_bits)):
        for i in range(nb >> (t + 1)):
            part_copy(t, i).wait_send()
    out_ref[0 : full.shape[0], :] = full[...]
    out_ref[full.shape[0] :, :] = rhs_sum[...]


def observe(obs_n, state_n, ids, counts, cells, mean_row, ops, readings, stds):
    nb = ops.shape[0]
    members = cells.shape[1]
    rows = packed_rows(members, obs_n * state_n)
    rounds = len(bits_of(state_n))
    steps = len(bits_of(obs_n)) + rounds
    hops = pltpu.SemaphoreType.DMA((2, obs_n - 1))
    dma = lambda *shape: pltpu.SemaphoreType.DMA(shape)
    return pl.pallas_call(
        functools.partial(observe_kernel, obs_n, state_n),
        out_shape=jax.ShapeDtypeStruct((rows + 8, BLK), jnp.float32),
        in_specs=[pl.BlockSpec(memory_space=pltpu.SMEM)] * 2
        + [pl.BlockSpec(memory_space=pl.ANY)] * 5,
        out_specs=pl.BlockSpec(memory_space=pltpu.VMEM),
        scratch_shapes=[
            pltpu.VMEM(mean_row.shape, jnp.float32),
            pltpu.VMEM(ops.shape, jnp.bfloat16),
            pltpu.VMEM((nb, BLK), jnp.float32),
            pltpu.VMEM((nb, BLK), jnp.float32),
            dma(5),
            pltpu.VMEM((obs_n, BLK, members), jnp.bfloat16),
            pltpu.VMEM((obs_n, 16, BLK), jnp.bfloat16),
            pltpu.VMEM((nb // state_n, BLK, members), jnp.float32),
            pltpu.VMEM((nb, BLK, members), jnp.bfloat16),
            pltpu.VMEM((nb, BLK, members), jnp.bfloat16),
            pltpu.VMEM((nb, BLK), jnp.float32),
            pltpu.VMEM((rounds, nb, BLK), jnp.float32),
            pltpu.VMEM((rows, BLK), jnp.float32),
            pltpu.VMEM((rows, BLK), jnp.float32),
            pltpu.VMEM((rows, BLK), jnp.float32),
            pltpu.VMEM((8, BLK), jnp.float32),
            pltpu.VMEM((steps, 8, BLK), jnp.float32),
            hops, hops, hops, hops,
            dma(nb), dma(nb), dma(rounds), dma(rounds),
            dma(2, 2 * steps), dma(2, 2 * steps), dma(steps), dma(steps),
        ],
        compiler_params=pltpu.CompilerParams(
            collective_id=0, has_side_effects=True, vmem_limit_bytes=60 << 20
        ),
    )(ids, counts, cells, mean_row, ops, readings, stds)


MESH = pl.DeviceIdType.MESH


def fused_kernel(
    obs_n, state_n, ids_ref, counts_ref, cells_hbm, mean_hbm, ops_hbm, read_hbm, std_hbm, out_ref,
    mean_row, ops_ref, read_ref, std_ref, load_sem,
    slab, slab_mean, part, sent, got, inno, inno_got, acc, core_got, first_got, piece_got, full,
    rhs_sum, rhs_got,
    slab_send, slab_recv, mean_send, mean_recv, part_send, part_recv, inno_send, inno_recv,
    core_send, core_recv, sum_send, sum_recv, all_send, all_recv, rhs_send, rhs_recv,
):
    me_o, me_s = lax.axis_index("obs"), lax.axis_index("state")
    nb, slots = ops_ref.shape[0], ops_ref.shape[1]
    members = slab.shape[2]
    blocks = members // BLK
    state_bits = bits_of(state_n)
    ways = obs_n * state_n
    chips = ways // 2
    me = me_o * state_n + me_s
    chip, core = me // 2, me % 2

    loads = [
        pltpu.make_async_copy(src, dst, load_sem.at[n])
        for n, (src, dst) in enumerate([
            (cells_hbm, slab.at[me_o]), (mean_hbm, mean_row), (read_hbm, read_ref),
            (std_hbm, std_ref), (ops_hbm, ops_ref),
        ])
    ]
    for load in loads:
        load.start()

    def place(index):
        index = lax.rem(index, ways)
        return {"obs": index // state_n, "state": lax.rem(index, state_n)}

    barrier = pltpu.get_barrier_semaphore()
    for d in range(1, ways):
        pl.semaphore_signal(barrier, inc=1, device_id=place(me + d), device_id_type=MESH)
    loads[0].wait()
    loads[1].wait()
    slab_mean[me_o] = jnp.broadcast_to(mean_row[...], (16, BLK)).astype(jnp.bfloat16)
    pl.semaphore_wait(barrier, ways - 1)

    def remote(src, dst, send, recv, where):
        return pltpu.make_async_remote_copy(
            src_ref=src, dst_ref=dst, send_sem=send, recv_sem=recv,
            device_id=where, device_id_type=MESH,
        )

    def clip(x):
        return jnp.clip(x, 0, obs_n - 1)

    half_rows = BLK // 2

    def slab_copy(block, slot, h, to):
        rows = pl.ds(h * half_rows, half_rows)
        return remote(
            slab.at[block, rows], slab.at[block, rows],
            slab_send.at[slot, h], slab_recv.at[block, h], {"obs": to},
        )

    def mean_copy(block, slot, to):
        return remote(
            slab_mean.at[block], slab_mean.at[block],
            mean_send.at[slot], mean_recv.at[block], {"obs": to},
        )

    reach = [2, -2, 1, -1]
    far = [3, -3] + reach

    def inside(delta):
        return (me_o + delta >= 0) & (me_o + delta <= obs_n - 1)

    for slot, delta in enumerate(reach):
        @pl.when(inside(delta))
        def _():
            for h in range(2):
                slab_copy(me_o, slot, h, clip(me_o + delta)).start()
    for slot, delta in enumerate(far):
        @pl.when(inside(delta))
        def _():
            mean_copy(me_o, slot, clip(me_o + delta)).start()
    relays = [(2, 0, 3), (1, 3, 0)]
    for at, block, to in relays:
        @pl.when(me_o == at)
        def _():
            for h in range(2):
                slab_copy(block, 4, h, to).wait_recv()
                slab_copy(block, 4, h, to).start()

    for load in loads[2:]:
        load.wait()
    for block in range(obs_n):
        @pl.when(me_o != block)
        def _():
            mean_copy(block, 0, 0).wait_recv()
    lane = lax.broadcasted_iota(jnp.int32, (1, BLK), 1)

    def weight_of(b):
        return jnp.where(lane < counts_ref[b], 1.0 / std_ref[pl.ds(b, 1), :], 0.0)

    @pl.loop(0, nb)
    def _(b):
        mean = jnp.zeros((16, BLK), jnp.float32)
        for j in range(slots):
            mean += lax.dot_general(
                slab_mean[ids_ref[b, j]], ops_ref[b, j], NT, preferred_element_type=jnp.float32
            )
        share = read_ref[pl.ds(b, 1), :] * (1.0 / state_n)
        inno[pl.ds(b, 1), :] = weight_of(b) * (share - mean[0:1])

    def partner(bit):
        return me_s + bit - 2 * bit * ((me_s // bit) % 2)

    def inno_copy(t):
        where = {"state": partner(state_bits[t])}
        return remote(inno, inno_got.at[t], inno_send.at[t], inno_recv.at[t], where)

    inno_copy(0).start()
    for block in range(obs_n):
        relayed = me_o != block
        for at, source, _ in relays:
            if source == block:
                relayed = relayed & (me_o != at)

        @pl.when(relayed)
        def _():
            for h in range(2):
                slab_copy(block, 0, h, 0).wait_recv()

    def observe(b):
        rows = jnp.zeros((BLK, members), jnp.float32)
        for j in range(slots):
            rows += jnp.dot(ops_ref[b, j], slab[ids_ref[b, j]], preferred_element_type=jnp.float32)
        return rows * jnp.broadcast_to(weight_of(b), (BLK, BLK)).T[:, 0:1]

    def part_copy(t, i):
        n = nb - (nb >> t) + i
        where = {"state": partner(state_bits[t])}
        return remote(sent.at[n], got.at[n], part_send.at[n], part_recv.at[n], where)

    lows = [0]
    for t, bit in enumerate(state_bits):
        half = nb >> (t + 1)
        keep = (me_s // bit) % 2 * half
        give = lows[-1] + half - keep
        lows.append(lows[-1] + keep)

        def total(b, upto):
            value = observe(b)
            for u in range(upto):
                part_copy(u, b - lows[u + 1]).wait_recv()
                value += got[nb - (nb >> u) + b - lows[u + 1]].astype(jnp.float32)
            return value

        @pl.loop(0, half)
        def _(i):
            sent[nb - (nb >> t) + i] = total(give + i, t).astype(jnp.bfloat16)
            part_copy(t, i).start()

        inno_copy(t).wait()
        inno[...] += inno_got[t]
        if t + 1 < len(state_bits):
            inno_copy(t + 1).start()
    own = nb // state_n
    low = lows[-1]
    last = len(state_bits) - 1

    @pl.loop(0, own)
    def _(i):
        value = observe(low + i)
        for u in range(last):
            part_copy(u, low + i - lows[u + 1]).wait_recv()
            value += got[nb - (nb >> u) + low + i - lows[u + 1]].astype(jnp.float32)
        part[i] = value

    @pl.loop(0, own)
    def _(i):
        part_copy(last, i).wait_recv()
        part[i] += got[nb - (nb >> last) + i].astype(jnp.float32)

    rows = [(i + 1) * BLK for i in range(blocks)]
    base = [sum(rows[:i]) for i in range(blocks)]
    piece = [r // ways for r in rows]
    core_at = [(base[i] - base[1]) // 2 if i else 0 for i in range(blocks)]
    piece_at = [sum(piece[1:i]) for i in range(blocks)]
    scaled = part[...].reshape(own * BLK, members)
    both = split(scaled)

    def columns(i, count):
        return [x[:, i * BLK : (i + count) * BLK] for x in both]

    def gram_row(i):
        result = transposed_times(columns(i, 1), columns(0, i + 1))
        for j in range(i + 1):
            acc[base[i] + j * BLK : base[i] + (j + 1) * BLK, :] = result[:, j * BLK : (j + 1) * BLK]

    def all_pieces(i):
        at = base[i] + core * (rows[i] // 2) + chip * piece[i] if i else me * piece[0]
        return pl.ds(pl.multiple_of(at, 8), piece[i])

    def first_copy(d):
        target = lax.rem(me + d, ways)
        return remote(
            acc.at[pl.ds(pl.multiple_of(target * piece[0], 8), piece[0])], first_got.at[d - 1],
            sum_send.at[0], sum_recv.at[0], place(me + d),
        )

    def core_copy(i):
        count = rows[i] // 2
        return remote(
            acc.at[pl.ds(pl.multiple_of(base[i] + (1 - core) * count, 8), count)],
            core_got.at[pl.ds(core_at[i], count)],
            core_send.at[i], core_recv.at[i], {"state": partner(1)},
        )

    def sum_copy(i, d):
        target = lax.rem(chip + d, chips)
        at = base[i] + core * (rows[i] // 2) + target * piece[i]
        return remote(
            acc.at[pl.ds(pl.multiple_of(at, 8), piece[i])],
            piece_got.at[d - 1, pl.ds(piece_at[i], piece[i])],
            sum_send.at[i], sum_recv.at[i], place(target * 2 + core),
        )

    def all_copy(i, d):
        return remote(
            full.at[all_pieces(i)], full.at[all_pieces(i)],
            all_send.at[i], all_recv.at[i], place(me + d),
        )

    def rhs_copy(d):
        return remote(
            rhs_sum, rhs_got.at[d - 1], rhs_send.at[0], rhs_recv.at[0], place(me + d)
        )

    def whole_first():
        return remote(first_got, first_got, sum_send.at[0], sum_recv.at[0], place(me + 1))

    def whole_sum(i):
        ref = piece_got.at[:, pl.ds(piece_at[i], piece[i])]
        return remote(ref, ref, sum_send.at[i], sum_recv.at[i], place(me + 1))

    def whole_all(i):
        ref = full.at[pl.ds(base[i], (ways - 1) * piece[i])]
        return remote(ref, ref, all_send.at[i], all_recv.at[i], place(me + 1))

    def whole_rhs():
        return remote(rhs_got, rhs_got, rhs_send.at[0], rhs_recv.at[0], place(me + 1))

    gram_row(0)
    for d in range(1, ways):
        first_copy(d).start()
    for i in range(1, blocks):
        gram_row(i)
        core_copy(i).start()
    seen = [inno[pl.ds(low + i, 1), :] for i in range(own)]
    seen = split(jnp.broadcast_to(jnp.concatenate(seen, axis=1), (16, own * BLK)))
    rhs = lax.dot_general(
        jnp.concatenate([seen[0], seen[0], seen[1]], axis=1),
        jnp.concatenate([both[0], both[1], both[0]], axis=0),
        (((1,), (0,)), ((), ())), preferred_element_type=jnp.float32,
    )
    rhs_sum[...] = jnp.zeros((8, BLK), jnp.float32)
    for j in range(blocks):
        rhs_sum[j : j + 1, :] = rhs[0:1, j * BLK : (j + 1) * BLK]
    for i in range(1, blocks):
        core_copy(i).wait_recv()
        mine = pl.ds(pl.multiple_of(base[i] + core * (rows[i] // 2), 8), rows[i] // 2)
        acc[mine, :] += core_got[core_at[i] : core_at[i] + rows[i] // 2, :]
        for d in range(1, chips):
            sum_copy(i, d).start()
    for d in range(1, ways):
        rhs_copy(d).start()

    def gather_row(i):
        if i:
            whole_sum(i).wait_recv()
        else:
            whole_first().wait_recv()
        value = acc[all_pieces(i), :]
        for d in range(1, chips if i else ways):
            if i:
                value += piece_got[d - 1, piece_at[i] : piece_at[i] + piece[i], :]
            else:
                value += first_got[d - 1]
        full[all_pieces(i), :] = value
        for d in range(1, ways):
            all_copy(i, d).start()

    row = lax.broadcasted_iota(jnp.int32, (BLK, BLK), 0)
    col = lax.broadcasted_iota(jnp.int32, (BLK, BLK), 1)
    ridge = jnp.where(row == col, members - 1.0, 0.0)

    def block_of(i, j):
        value = full[base[i] + j * BLK : base[i] + (j + 1) * BLK, :]
        return value + ridge if i == j else value

    ncells = slab.shape[1]
    inverse, factor, solved, solved_split = [], {}, [], []

    def reduced(value, parts, i):
        if not parts:
            return value
        x = [jnp.concatenate([p[n] for p in parts], axis=1) for n in range(2)]
        y = [jnp.concatenate([factor[i, m][n] for m in range(len(parts))], axis=1) for n in range(2)]
        return value - times_transposed(x, y)

    def solve(i):
        value = slab[me_o, :, i * BLK : (i + 1) * BLK].astype(jnp.float32)
        value = reduced(value, solved_split, i)
        solved.append(times_transposed(split(value), inverse[i]))
        solved_split.append(split(solved[i]))

    gather_row(0)
    gather_row(1)
    whole_all(0).wait_recv()
    if blocks > 2:
        gather_row(2)
    for i in range(blocks):
        if i:
            whole_all(i).wait_recv()
            for k in range(i):
                value = reduced(block_of(i, k), [factor[i, m] for m in range(k)], k)
                factor[i, k] = split(times_transposed(split(value), inverse[k]))
            solve(i - 1)
        value = block_of(i, i)
        if i:
            value = reduced(value, [factor[i, m] for m in range(i)], i)
        inverse.append(split(inverse_factor(value)))
        if i + 3 < blocks:
            gather_row(i + 3)
    whole_rhs().wait_recv()
    total_rhs = rhs_sum[...]
    for d in range(1, ways):
        total_rhs += rhs_got[d - 1]
    solve(blocks - 1)
    middle, middle_split = [], []
    for i in range(blocks):
        value = jnp.broadcast_to(total_rhs[i : i + 1, :], (16, BLK))
        value = reduced(value, middle_split, i)
        middle.append(times_transposed(split(value), inverse[i]))
        middle_split.append(split(middle[i]))
    shift = jnp.zeros((ncells, 1), jnp.float32)
    for i in range(blocks):
        shift += jnp.sum(solved[i] * middle[i][0:1], axis=1, keepdims=True)
    root = (members - 1.0) ** 0.5
    offset = jnp.broadcast_to(mean_row[...], (BLK, ncells)).T[:, 0:1] + shift
    for i in range(blocks):
        out_ref[:, i * BLK : (i + 1) * BLK] = (offset + root * solved[i]).astype(jnp.bfloat16)

    for slot, delta in enumerate(reach):
        @pl.when(inside(delta))
        def _():
            for h in range(2):
                slab_copy(me_o, slot, h, clip(me_o + delta)).wait_send()
    for slot, delta in enumerate(far):
        @pl.when(inside(delta))
        def _():
            mean_copy(me_o, slot, clip(me_o + delta)).wait_send()
    for at, block, to in relays:
        @pl.when(me_o == at)
        def _():
            for h in range(2):
                slab_copy(block, 4, h, to).wait_send()
    for t in range(len(state_bits)):
        for i in range(nb >> (t + 1)):
            part_copy(t, i).wait_send()
    whole_first().wait_send()
    whole_rhs().wait_send()
    whole_all(0).wait_send()
    for i in range(1, blocks):
        core_copy(i).wait_send()
        whole_sum(i).wait_send()
        whole_all(i).wait_send()


def fused(obs_n, state_n, ids, counts, cells, mean_row, ops, readings, stds):
    nb = ops.shape[0]
    members = cells.shape[1]
    blocks = members // BLK
    ways = obs_n * state_n
    total = BLK * blocks * (blocks + 1) // 2
    rounds = len(bits_of(state_n))
    dma = lambda *shape: pltpu.SemaphoreType.DMA(shape)
    return pl.pallas_call(
        functools.partial(fused_kernel, obs_n, state_n),
        out_shape=jax.ShapeDtypeStruct(cells.shape, jnp.bfloat16),
        in_specs=[pl.BlockSpec(memory_space=pltpu.SMEM)] * 2
        + [pl.BlockSpec(memory_space=pl.ANY)] * 5,
        out_specs=pl.BlockSpec(memory_space=pltpu.VMEM),
        scratch_shapes=[
            pltpu.VMEM(mean_row.shape, jnp.float32),
            pltpu.VMEM(ops.shape, jnp.bfloat16),
            pltpu.VMEM((nb, BLK), jnp.float32),
            pltpu.VMEM((nb, BLK), jnp.float32),
            dma(5),
            pltpu.VMEM((obs_n, BLK, members), jnp.bfloat16),
            pltpu.VMEM((obs_n, 16, BLK), jnp.bfloat16),
            pltpu.VMEM((nb // state_n, BLK, members), jnp.float32),
            pltpu.VMEM((nb, BLK, members), jnp.bfloat16),
            pltpu.VMEM((nb, BLK, members), jnp.bfloat16),
            pltpu.VMEM((nb, BLK), jnp.float32),
            pltpu.VMEM((rounds, nb, BLK), jnp.float32),
            pltpu.VMEM((total, BLK), jnp.float32),
            pltpu.VMEM(((total - BLK) // 2, BLK), jnp.float32),
            pltpu.VMEM((ways - 1, BLK // ways, BLK), jnp.float32),
            pltpu.VMEM((ways // 2 - 1, (total - BLK) // ways, BLK), jnp.float32),
            pltpu.VMEM((total, BLK), jnp.float32),
            pltpu.VMEM((8, BLK), jnp.float32),
            pltpu.VMEM((ways - 1, 8, BLK), jnp.float32),
            dma(5, 2), dma(obs_n, 2), dma(6), dma(obs_n),
            dma(nb), dma(nb), dma(rounds), dma(rounds),
            dma(blocks), dma(blocks), dma(blocks), dma(blocks), dma(blocks), dma(blocks),
            dma(1), dma(1),
        ],
        compiler_params=pltpu.CompilerParams(
            collective_id=0, has_side_effects=True, vmem_limit_bytes=60 << 20
        ),
    )(ids, counts, cells, mean_row, ops, readings, stds)


def local(
    obs_n,
    state_n,
    anomalies,
    prior_ensemble_mean,
    operator_blocks,
    block_column_ids,
    observation_counts,
    observed_readings,
    observation_error_std,
):
    cells = anomalies[0]
    if obs_n == 4 and state_n == 4 and 1 < cells.shape[1] // BLK <= 8:
        return fused(
            obs_n, state_n, block_column_ids[:, 0], observation_counts, cells, prior_ensemble_mean,
            operator_blocks[:, 0], observed_readings, observation_error_std,
        )[None]
    packed = observe(
        obs_n, state_n, block_column_ids[:, 0], observation_counts, cells, prior_ensemble_mean,
        operator_blocks[:, 0], observed_readings, observation_error_std,
    )
    return finish(packed, cells, prior_ensemble_mean)[None]


def solution(mesh):
    placed = (
        P("state", "obs", None),
        P("state", "obs"),
        P(("net", "obs"), "state", None, None, None),
        P(("net", "obs"), "state", None),
        P(("net", "obs")),
        P(("net", "obs"), None),
        P(("net", "obs"), None),
    )
    return jax.shard_map(
        functools.partial(local, mesh.shape["obs"], mesh.shape["state"]),
        mesh=mesh,
        in_specs=placed,
        out_specs=P(("net", "state"), "obs", None),
        check_vma=False,
    )
```

```python
import functools
import jax
import jax.numpy as jnp
from jax import lax
from jax.experimental import pallas as pl
from jax.experimental.pallas import tpu as pltpu
from jax.sharding import PartitionSpec as P

BLK = 128
HI = lax.Precision.HIGHEST
NT = (((1,), (1,)), ((), ()))


TN = (((0,), (0,)), ((), ()))


def split(x):
    high = x.astype(jnp.bfloat16)
    return high, (x - high.astype(jnp.float32)).astype(jnp.bfloat16)


def joined(x, y, axis, dims):
    (xh, xl), (yh, yl) = x, y
    return lax.dot_general(
        jnp.concatenate([xh, xh, xl], axis=axis), jnp.concatenate([yh, yl, yh], axis=axis), dims,
        preferred_element_type=jnp.float32,
    )


def times_transposed(x, y):
    return joined(x, y, 1, NT)


def transposed_times(x, y):
    return joined(x, y, 0, TN)


def inverse_factor(block, width=32, between=None):
    row = lax.broadcasted_iota(jnp.int32, (BLK, BLK), 0)
    col = lax.broadcasted_iota(jnp.int32, (BLK, BLK), 1)
    eye = (row == col).astype(jnp.float32)
    groups = BLK // 8
    left = [block[8 * g : 8 * g + 8] for g in range(groups)]
    right = [eye[8 * g : 8 * g + 8] for g in range(groups)]
    sub = lax.broadcasted_iota(jnp.int32, (8, 1), 0)
    lane = lax.broadcasted_iota(jnp.int32, (1, BLK), 1)
    local = width // 8
    for start in range(0, BLK, width):
        if between:
            between(start // width)
        g0 = start // 8
        spread = [
            [
                None if h < j // 8
                else jnp.broadcast_to(left[g0 + h][:, start + j : start + j + 1], (8, BLK))
                for h in range(local)
            ]
            for j in range(width)
        ]
        scaled = []
        roots = []
        for j in range(width):
            gj, ij = divmod(j, 8)
            pivot = spread[j][gj][ij : ij + 1]
            inv = 1.0 / pivot
            roots.append(lax.rsqrt(pivot))
            lrow = left[g0 + gj][ij : ij + 1]
            rrow = right[g0 + gj][ij : ij + 1]
            scaled.append(lrow * inv)
            ms = {}
            for h in range(gj, local):
                m = spread[j][h]
                if h == gj:
                    if ij == 7:
                        continue
                    m = jnp.where(sub > ij, m, 0.0)
                ms[h] = m * inv
            for t in range(j + 1, width):
                gt, it = divmod(t, 8)
                shared = spread[j][gt][it : it + 1]
                for h in range(gt, local):
                    if h in ms:
                        spread[t][h] = spread[t][h] - ms[h] * shared
            for h in ms:
                left[g0 + h] = left[g0 + h] - ms[h] * lrow
                right[g0 + h] = right[g0 + h] - ms[h] * rrow
        upper_l = jnp.concatenate(left[g0 : g0 + local], axis=0)
        upper_r = jnp.concatenate(right[g0 : g0 + local], axis=0)
        end = start + width
        if end < BLK:
            low = jnp.where(lane >= end, jnp.concatenate(scaled, axis=0), 0.0)
            change = transposed_times(
                split(low), split(jnp.concatenate([upper_l, upper_r], axis=1))
            )
            for h in range(end // 8, groups):
                left[h] = left[h] - change[8 * h : 8 * h + 8, :BLK]
                right[h] = right[h] - change[8 * h : 8 * h + 8, BLK:]
        scale = jnp.concatenate(roots, axis=0)
        for h in range(local):
            right[g0 + h] = right[g0 + h] * scale[8 * h : 8 * h + 8]
    return jnp.concatenate(right, axis=0)


def finish_kernel(packed_ref, anom_ref, mean_ref, out_ref, work):
    cells, members = anom_ref.shape
    total = members + cells + 8
    row = lax.broadcasted_iota(jnp.int32, (BLK, BLK), 0)
    col = lax.broadcasted_iota(jnp.int32, (BLK, BLK), 1)
    ridge = jnp.where(row == col, members - 1.0, 0.0)
    start = 0
    last = packed_ref.shape[0] - 8
    for j in range(members // BLK):
        size = members - j * BLK
        cols = slice(j * BLK, (j + 1) * BLK)
        if j:
            work[0 : j * BLK, cols] = jnp.zeros((j * BLK, BLK), jnp.float32)
        work[cols, cols] = packed_ref[start : start + BLK, :] + ridge
        if size > BLK:
            work[(j + 1) * BLK : members, cols] = packed_ref[start + BLK : start + size, :]
        start += size
    for j in range(members // BLK):
        cols = slice(j * BLK, (j + 1) * BLK)
        work[members + cells : total, cols] = jnp.broadcast_to(
            packed_ref[last + j : last + j + 1, :], (8, BLK)
        )
    work[members : members + cells, :] = anom_ref[...].astype(jnp.float32)

    for off in range(0, members, BLK):
        end = off + BLK
        inv = inverse_factor(work[off:end, off:end])
        x = lax.dot_general(
            work[end:total, off:end], inv, NT, precision=HI, preferred_element_type=jnp.float32
        )
        work[members:total, off:end] = x[members - end :]
        if end < members:
            work[end : end + BLK, end : end + BLK] -= lax.dot_general(
                x[:BLK], x[:BLK], NT, precision=HI, preferred_element_type=jnp.float32
            )
            work[end + BLK : total, end : end + BLK] -= lax.dot_general(
                x[BLK:], x[:BLK], NT, precision=HI, preferred_element_type=jnp.float32
            )
        for at in range(end + BLK, members, BLK):
            work[at:total, at : at + BLK] -= lax.dot_general(
                x[at - end :], x[at - end : at - end + BLK], NT, precision=HI,
                preferred_element_type=jnp.float32,
            )

    solved = work[members : members + cells, :]
    shift = jnp.sum(solved * work[members + cells : members + cells + 1, :], axis=1, keepdims=True)
    root = (members - 1.0) ** 0.5
    mean = jnp.broadcast_to(mean_ref[...], (BLK, cells)).T[:, 0:1]
    out_ref[...] = (mean + (root * solved + shift)).astype(jnp.bfloat16)


def finish(packed, cells, mean_row):
    ncells, members = cells.shape
    return pl.pallas_call(
        finish_kernel,
        out_shape=jax.ShapeDtypeStruct((ncells, members), jnp.bfloat16),
        in_specs=[pl.BlockSpec(memory_space=pltpu.VMEM)] * 3,
        out_specs=pl.BlockSpec(memory_space=pltpu.VMEM),
        scratch_shapes=[pltpu.VMEM((members + ncells + 8, members), jnp.float32)],
        compiler_params=pltpu.CompilerParams(vmem_limit_bytes=32 << 20),
    )(packed, cells, mean_row)


def packed_rows(members, ways):
    need = sum(members - j * BLK for j in range(members // BLK))
    step = 16 * ways
    return (need + step - 1) // step * step


def bits_of(n):
    return [1 << t for t in range(n.bit_length() - 1)]


def observe_kernel(
    obs_n, state_n, ids_ref, counts_ref, cells_hbm, mean_hbm, ops_hbm, read_hbm, std_hbm, out_ref,
    mean_row, ops_ref, read_ref, std_ref, load_sem,
    slab, slab_mean, part, sent, got, inno, inno_got, acc, acc_got, full, rhs_sum, rhs_got,
    right_send, right_recv, left_send, left_recv, part_send, part_recv, inno_send, inno_recv,
    acc_send, acc_recv, rhs_send, rhs_recv,
):
    me_o, me_s = lax.axis_index("obs"), lax.axis_index("state")
    nb, slots = ops_ref.shape[0], ops_ref.shape[1]
    members = slab.shape[2]
    state_bits, obs_bits = bits_of(state_n), bits_of(obs_n)

    loads = [
        pltpu.make_async_copy(src, dst, load_sem.at[n])
        for n, (src, dst) in enumerate([
            (cells_hbm, slab.at[me_o]), (mean_hbm, mean_row), (read_hbm, read_ref),
            (std_hbm, std_ref), (ops_hbm, ops_ref),
        ])
    ]
    for load in loads:
        load.start()

    def partner(axis, bit):
        me = me_s if axis == "state" else me_o
        return me + bit - 2 * bit * ((me // bit) % 2)

    barrier = pltpu.get_barrier_semaphore()
    greeted = [{"obs": lax.rem(me_o + 1, obs_n)}, {"obs": lax.rem(me_o + obs_n - 1, obs_n)}]
    greeted += [{"obs": partner("obs", b)} for b in obs_bits]
    greeted += [{"state": partner("state", b)} for b in state_bits]
    for where in greeted:
        pl.semaphore_signal(barrier, inc=1, device_id=where, device_id_type=pl.DeviceIdType.MESH)
    loads[0].wait()
    loads[1].wait()
    slab_mean[me_o] = jnp.broadcast_to(mean_row[...], (16, BLK)).astype(jnp.bfloat16)
    pl.semaphore_wait(barrier, len(greeted))

    def remote(src, dst, send, recv, where):
        return pltpu.make_async_remote_copy(
            src_ref=src, dst_ref=dst, send_sem=send, recv_sem=recv,
            device_id=where, device_id_type=pl.DeviceIdType.MESH,
        )

    def hop(block, sends, recvs, t, to):
        return [
            remote(slab.at[block], slab.at[block], sends.at[0, t], recvs.at[0, t], {"obs": to}),
            remote(slab_mean.at[block], slab_mean.at[block], sends.at[1, t], recvs.at[1, t], {"obs": to}),
        ]

    def clip(x):
        return jnp.clip(x, 0, obs_n - 1)

    for t in range(obs_n - 1):
        @pl.when((me_o < obs_n - 1) & (me_o - t >= 0))
        def _():
            for c in hop(clip(me_o - t), right_send, right_recv, t, clip(me_o + 1)):
                c.start()

        @pl.when((me_o > 0) & (me_o + t <= obs_n - 1))
        def _():
            for c in hop(clip(me_o + t), left_send, left_recv, t, clip(me_o - 1)):
                c.start()

        @pl.when(me_o - 1 - t >= 0)
        def _():
            for c in hop(clip(me_o - 1 - t), right_send, right_recv, t, clip(me_o - 1)):
                c.wait_recv()

        @pl.when(me_o + 1 + t <= obs_n - 1)
        def _():
            for c in hop(clip(me_o + 1 + t), left_send, left_recv, t, clip(me_o + 1)):
                c.wait_recv()

    for load in loads[2:]:
        load.wait()
    lane = lax.broadcasted_iota(jnp.int32, (1, BLK), 1)

    def weight_of(b):
        return jnp.where(lane < counts_ref[b], 1.0 / std_ref[pl.ds(b, 1), :], 0.0)

    @pl.loop(0, nb)
    def _(b):
        mean = jnp.zeros((16, BLK), jnp.float32)
        for j in range(slots):
            mean += lax.dot_general(
                slab_mean[ids_ref[b, j]], ops_ref[b, j], NT, preferred_element_type=jnp.float32
            )
        share = read_ref[pl.ds(b, 1), :] * (1.0 / state_n)
        inno[pl.ds(b, 1), :] = weight_of(b) * (share - mean[0:1])

    def inno_copy(t):
        where = {"state": partner("state", state_bits[t])}
        return remote(inno, inno_got.at[t], inno_send.at[t], inno_recv.at[t], where)

    inno_copy(0).start()

    def observe(b):
        rows = jnp.zeros((BLK, members), jnp.float32)
        for j in range(slots):
            rows += jnp.dot(ops_ref[b, j], slab[ids_ref[b, j]], preferred_element_type=jnp.float32)
        return rows * jnp.broadcast_to(weight_of(b), (BLK, BLK)).T[:, 0:1]

    def part_copy(t, i):
        n = nb - (nb >> t) + i
        where = {"state": partner("state", state_bits[t])}
        return remote(sent.at[n], got.at[n], part_send.at[n], part_recv.at[n], where)

    lows = [0]
    for t, bit in enumerate(state_bits):
        half = nb >> (t + 1)
        keep = (me_s // bit) % 2 * half
        give = lows[-1] + half - keep
        lows.append(lows[-1] + keep)

        def total(b, upto):
            value = observe(b)
            for u in range(upto):
                part_copy(u, b - lows[u + 1]).wait_recv()
                value += got[nb - (nb >> u) + b - lows[u + 1]].astype(jnp.float32)
            return value

        @pl.loop(0, half)
        def _(i):
            sent[nb - (nb >> t) + i] = total(give + i, t).astype(jnp.bfloat16)
            part_copy(t, i).start()

        inno_copy(t).wait()
        inno[...] += inno_got[t]
        if t + 1 < len(state_bits):
            inno_copy(t + 1).start()
    own = nb // state_n
    low = lows[-1]
    last = len(state_bits) - 1

    @pl.loop(0, own)
    def _(i):
        value = observe(low + i)
        for u in range(last):
            part_copy(u, low + i - lows[u + 1]).wait_recv()
            value += got[nb - (nb >> u) + low + i - lows[u + 1]].astype(jnp.float32)
        part[i] = value

    @pl.loop(0, own)
    def _(i):
        part_copy(last, i).wait_recv()
        part[i] += got[nb - (nb >> last) + i].astype(jnp.float32)

    scaled = part[...].reshape(own * BLK, members)
    row = 0
    for j in range(members // BLK):
        size = members - j * BLK
        acc[row : row + size, :] = lax.dot_general(
            scaled[:, j * BLK :], scaled[:, j * BLK : (j + 1) * BLK], (((0,), (0,)), ((), ())),
            precision=HI, preferred_element_type=jnp.float32,
        )
        row += size
    if row < acc.shape[0]:
        acc[row:, :] = jnp.zeros((acc.shape[0] - row, BLK), jnp.float32)
    rhs = jnp.zeros((8, members), jnp.float32)
    for i in range(own):
        rhs += jnp.dot(
            jnp.broadcast_to(inno[pl.ds(low + i, 1), :], (8, BLK)), scaled[i * BLK : (i + 1) * BLK],
            precision=HI, preferred_element_type=jnp.float32,
        )
    rhs_sum[...] = jnp.zeros((8, BLK), jnp.float32)
    for j in range(members // BLK):
        rhs_sum[j : j + 1, :] = rhs[0:1, j * BLK : (j + 1) * BLK]

    by_state = [("state", b) for b in state_bits]
    by_obs = [("obs", b) for b in obs_bits]
    orders = [by_state + by_obs, by_state[:1] + by_obs + by_state[1:]]
    steps = len(orders[0])
    size = acc.shape[0] // 2
    bases = [0, size]
    spots = [0, size]
    trail = []
    for n in range(steps):
        size //= 2
        copies = []
        for k in range(2):
            axis, bit = orders[k][n]
            keep = ((me_s if axis == "state" else me_o) // bit) % 2 * size
            where = {axis: partner(axis, bit)}
            give = pl.multiple_of(bases[k] + size - keep, 8)
            copies.append(remote(
                acc.at[pl.ds(give, size)], acc_got.at[pl.ds(spots[k], size)],
                acc_send.at[k, n], acc_recv.at[k, n], where,
            ))
            bases[k] = pl.multiple_of(bases[k] + keep, 8)
            trail.append((k, n, where, bases[k], size))
            if k == 0:
                copies.append(remote(rhs_sum, rhs_got.at[n], rhs_send.at[n], rhs_recv.at[n], where))
        for copy in copies:
            copy.start()
        for copy in copies:
            copy.wait()
        for k in range(2):
            acc[pl.ds(bases[k], size), :] += acc_got[spots[k] : spots[k] + size, :]
            spots[k] += size
        rhs_sum[...] += rhs_got[n]
    for k in range(2):
        full[pl.ds(bases[k], size), :] = acc[pl.ds(bases[k], size), :]
    for n in reversed(range(steps)):
        copies = [
            remote(
                full.at[pl.ds(base, size)], full.at[pl.ds(base, size)],
                acc_send.at[k, steps + n], acc_recv.at[k, steps + n], where,
            )
            for k, m, where, base, size in trail if m == n
        ]
        for copy in copies:
            copy.start()
        for copy in copies:
            copy.wait()

    for t in range(obs_n - 1):
        @pl.when((me_o < obs_n - 1) & (me_o - t >= 0))
        def _():
            for c in hop(clip(me_o - t), right_send, right_recv, t, clip(me_o + 1)):
                c.wait_send()

        @pl.when((me_o > 0) & (me_o + t <= obs_n - 1))
        def _():
            for c in hop(clip(me_o + t), left_send, left_recv, t, clip(me_o - 1)):
                c.wait_send()
    for t in range(len(state_bits)):
        for i in range(nb >> (t + 1)):
            part_copy(t, i).wait_send()
    out_ref[0 : full.shape[0], :] = full[...]
    out_ref[full.shape[0] :, :] = rhs_sum[...]


def observe(obs_n, state_n, ids, counts, cells, mean_row, ops, readings, stds):
    nb = ops.shape[0]
    members = cells.shape[1]
    rows = packed_rows(members, obs_n * state_n)
    rounds = len(bits_of(state_n))
    steps = len(bits_of(obs_n)) + rounds
    hops = pltpu.SemaphoreType.DMA((2, obs_n - 1))
    dma = lambda *shape: pltpu.SemaphoreType.DMA(shape)
    return pl.pallas_call(
        functools.partial(observe_kernel, obs_n, state_n),
        out_shape=jax.ShapeDtypeStruct((rows + 8, BLK), jnp.float32),
        in_specs=[pl.BlockSpec(memory_space=pltpu.SMEM)] * 2
        + [pl.BlockSpec(memory_space=pl.ANY)] * 5,
        out_specs=pl.BlockSpec(memory_space=pltpu.VMEM),
        scratch_shapes=[
            pltpu.VMEM(mean_row.shape, jnp.float32),
            pltpu.VMEM(ops.shape, jnp.bfloat16),
            pltpu.VMEM((nb, BLK), jnp.float32),
            pltpu.VMEM((nb, BLK), jnp.float32),
            dma(5),
            pltpu.VMEM((obs_n, BLK, members), jnp.bfloat16),
            pltpu.VMEM((obs_n, 16, BLK), jnp.bfloat16),
            pltpu.VMEM((nb // state_n, BLK, members), jnp.float32),
            pltpu.VMEM((nb, BLK, members), jnp.bfloat16),
            pltpu.VMEM((nb, BLK, members), jnp.bfloat16),
            pltpu.VMEM((nb, BLK), jnp.float32),
            pltpu.VMEM((rounds, nb, BLK), jnp.float32),
            pltpu.VMEM((rows, BLK), jnp.float32),
            pltpu.VMEM((rows, BLK), jnp.float32),
            pltpu.VMEM((rows, BLK), jnp.float32),
            pltpu.VMEM((8, BLK), jnp.float32),
            pltpu.VMEM((steps, 8, BLK), jnp.float32),
            hops, hops, hops, hops,
            dma(nb), dma(nb), dma(rounds), dma(rounds),
            dma(2, 2 * steps), dma(2, 2 * steps), dma(steps), dma(steps),
        ],
        compiler_params=pltpu.CompilerParams(
            collective_id=0, has_side_effects=True, vmem_limit_bytes=60 << 20
        ),
    )(ids, counts, cells, mean_row, ops, readings, stds)


MESH = pl.DeviceIdType.MESH


def fused_kernel(
    obs_n, state_n, ids_ref, counts_ref, cells_hbm, mean_hbm, ops_hbm, read_hbm, std_hbm, out_ref,
    mean_row, ops_ref, read_ref, std_ref, load_sem,
    slab, slab_mean, wide, seen, part, sent, got, inno, inno_got, acc, core_got, first_got,
    piece_got, full,
    slab_send, slab_recv, mean_send, mean_recv, part_send, part_recv, inno_send, inno_recv,
    core_send, core_recv, sum_send, sum_recv, all_send, all_recv, pass_send, pass_recv,
):
    me_o, me_s = lax.axis_index("obs"), lax.axis_index("state")
    nb, slots = ops_ref.shape[0], ops_ref.shape[1]
    members = slab.shape[2]
    blocks = members // BLK
    state_bits = bits_of(state_n)
    ways = obs_n * state_n
    chips = ways // 2
    me = me_o * state_n + me_s
    chip, core = me // 2, me % 2

    loads = [
        pltpu.make_async_copy(src, dst, load_sem.at[n])
        for n, (src, dst) in enumerate([
            (cells_hbm, slab.at[me_o]), (mean_hbm, mean_row), (read_hbm, read_ref),
            (std_hbm, std_ref), (ops_hbm, ops_ref),
        ])
    ]
    for load in loads:
        load.start()

    def place(index):
        index = lax.rem(index, ways)
        return {"obs": index // state_n, "state": lax.rem(index, state_n)}

    barrier = pltpu.get_barrier_semaphore()
    for d in range(1, ways):
        pl.semaphore_signal(barrier, inc=1, device_id=place(me + d), device_id_type=MESH)
    loads[0].wait()
    loads[1].wait()
    slab_mean[me_o] = jnp.broadcast_to(mean_row[...], (16, BLK)).astype(jnp.bfloat16)
    pl.semaphore_wait(barrier, ways - 1)

    def remote(src, dst, send, recv, where):
        return pltpu.make_async_remote_copy(
            src_ref=src, dst_ref=dst, send_sem=send, recv_sem=recv,
            device_id=where, device_id_type=MESH,
        )

    def clip(x):
        return jnp.clip(x, 0, obs_n - 1)

    half_rows = BLK // 2

    def slab_copy(block, slot, h, to):
        rows = pl.ds(h * half_rows, half_rows)
        return remote(
            slab.at[block, rows], slab.at[block, rows],
            slab_send.at[slot, h], slab_recv.at[block, h], {"obs": to},
        )

    def mean_copy(block, slot, to):
        return remote(
            slab_mean.at[block], slab_mean.at[block],
            mean_send.at[slot], mean_recv.at[block], {"obs": to},
        )

    reach = [2, -2, 1, -1]
    far = [3, -3] + reach

    def inside(delta):
        return (me_o + delta >= 0) & (me_o + delta <= obs_n - 1)

    for slot, delta in enumerate(far):
        @pl.when(inside(delta))
        def _():
            mean_copy(me_o, slot, clip(me_o + delta)).start()
    for slot, delta in enumerate(reach):
        @pl.when(inside(delta))
        def _():
            for h in range(2):
                slab_copy(me_o, slot, h, clip(me_o + delta)).start()
    relays = [(2, 0, 3), (1, 3, 0)]
    pad = acc.shape[0] - BLK
    acc[pad:, :] = jnp.zeros((BLK, BLK), jnp.float32)
    for load in loads[2:]:
        load.wait()
    lane = lax.broadcasted_iota(jnp.int32, (1, BLK), 1)

    def weight_of(b):
        return jnp.where(lane < counts_ref[b], 1.0 / std_ref[pl.ds(b, 1), :], 0.0)

    @pl.loop(0, nb)
    def _(b):
        weight = jnp.broadcast_to(weight_of(b), (BLK, BLK)).T
        at = pl.ds(pl.multiple_of(b * BLK, BLK), BLK)
        for half in range(2):
            some = slice(half * half_rows, (half + 1) * half_rows)
            columns = [jnp.zeros((half_rows, BLK), jnp.float32) for _ in range(obs_n)]
            for j in range(slots):
                block = ops_ref[b, j, some, :].astype(jnp.float32)
                for c in range(obs_n):
                    columns[c] += jnp.where(ids_ref[b, j] == c, block, 0.0)
            at = pl.ds(pl.multiple_of(b * BLK + half * half_rows, half_rows), half_rows)
            for c in range(obs_n):
                high, low = split(columns[c] * weight[some, :])
                wide[c, at, 0:BLK] = high
                wide[c, at, BLK : 2 * BLK] = low

    def observe(c, start, count, first):
        block = slab[c]
        at = pl.ds(start, count)
        for n in range(0, members, 2 * BLK):
            cut = slice(n, n + 2 * BLK)
            weights = block[:, cut]
            value = jnp.dot(
                wide[c, at, :], jnp.concatenate([weights, weights], axis=0),
                preferred_element_type=jnp.float32,
            )
            if first:
                seen[at, cut] = value
            else:
                seen[at, cut] += value

    observe(me_o, 0, nb * BLK, True)

    order = [(0, 1, 2, 3), (1, 0, 2, 3), (2, 3, 1, 0), (3, 2, 1, 0)]

    def met(k):
        return sum(jnp.where(me_o == o, order[o][k], 0) for o in range(obs_n))

    for at, block, to in relays:
        @pl.when(me_o == at)
        def _():
            for h in range(2):
                slab_copy(block, 4, h, to).wait_recv()
                slab_copy(block, 4, h, to).start()

    for block in range(obs_n):
        @pl.when(me_o != block)
        def _():
            mean_copy(block, 0, 0).wait_recv()

    @pl.loop(0, nb)
    def _(b):
        mean = jnp.zeros((16, BLK), jnp.float32)
        for j in range(slots):
            mean += lax.dot_general(
                slab_mean[ids_ref[b, j]], ops_ref[b, j], NT, preferred_element_type=jnp.float32
            )
        share = read_ref[pl.ds(b, 1), :] * (1.0 / state_n)
        inno[pl.ds(b, 1), :] = weight_of(b) * (share - mean[0:1])

    def partner(bit):
        return me_s + bit - 2 * bit * ((me_s // bit) % 2)

    def inno_copy(t):
        where = {"state": partner(state_bits[t])}
        return remote(inno, inno_got.at[t], inno_send.at[t], inno_recv.at[t], where)

    inno_copy(0).start()
    for n in range(1, obs_n - 1):
        for h in range(2):
            slab_copy(met(n), 0, h, 0).wait_recv()
        observe(met(n), 0, nb * BLK, False)
    relayed = me_o < 0
    for at, _, _ in relays:
        relayed = relayed | (me_o == at)

    @pl.when(jnp.logical_not(relayed))
    def _():
        for h in range(2):
            slab_copy(met(obs_n - 1), 0, h, 0).wait_recv()

    def rows_of(b):
        return seen[pl.ds(pl.multiple_of(b * BLK, BLK), BLK), :]

    def part_copy(t, i):
        n = nb - (nb >> t) + i
        where = {"state": partner(state_bits[t])}
        return remote(sent.at[n], got.at[n], part_send.at[n], part_recv.at[n], where)

    half = nb // 2
    keep = core * half
    for start in (half - keep, keep):
        observe(met(obs_n - 1), pl.multiple_of(start * BLK, BLK), half * BLK, False)
        if start is not keep:
            ahead = (1 - (me_s // 2) % 2) * (half // 2)

            @pl.loop(0, half)
            def _(n):
                i = lax.rem(n + ahead, half)
                sent[i] = rows_of(half - keep + i).astype(jnp.bfloat16)
                part_copy(0, i).start()

    lows = [0, keep]
    for t in range(1, len(state_bits)):
        half = nb >> (t + 1)
        keep = (me_s // state_bits[t]) % 2 * half
        give = lows[-1] + half - keep
        lows.append(lows[-1] + keep)

        @pl.loop(0, half)
        def _(i):
            value = rows_of(give + i)
            for u in range(t):
                part_copy(u, give + i - lows[u + 1]).wait_recv()
                value += got[nb - (nb >> u) + give + i - lows[u + 1]].astype(jnp.float32)
            sent[nb - (nb >> t) + i] = value.astype(jnp.bfloat16)
            part_copy(t, i).start()

    for t in range(len(state_bits)):
        inno_copy(t).wait()
        inno[...] += inno_got[t]
        if t + 1 < len(state_bits):
            inno_copy(t + 1).start()
    own = nb // state_n
    low = lows[-1]
    last = len(state_bits) - 1

    @pl.loop(0, own)
    def _(i):
        value = rows_of(low + i)
        for u in range(last):
            part_copy(u, low + i - lows[u + 1]).wait_recv()
            value += got[nb - (nb >> u) + low + i - lows[u + 1]].astype(jnp.float32)
        part[i] = value

    @pl.loop(0, own)
    def _(i):
        part_copy(last, i).wait_recv()
        part[i] += got[nb - (nb >> last) + i].astype(jnp.float32)

    rows = [(i + 1) * BLK + (BLK if i == blocks - 1 else 0) for i in range(blocks)]
    spread_rows = 1
    base = [sum(rows[:i]) for i in range(blocks)]
    piece = [r // ways for r in rows]
    core_at = [(base[i] - base[1]) // 2 if i else 0 for i in range(blocks)]
    piece_at = [sum(piece[1:i]) for i in range(blocks)]
    scaled = part[...].reshape(own * BLK, members)
    both = split(scaled)

    def columns(i, count):
        return [x[:, i * BLK : (i + count) * BLK] for x in both]

    def gram_row(i):
        result = transposed_times(columns(i, 1), columns(0, i + 1))
        for j in range(i + 1):
            acc[base[i] + j * BLK : base[i] + (j + 1) * BLK, :] = result[:, j * BLK : (j + 1) * BLK]

    def all_pieces(i):
        at = base[i] + core * (rows[i] // 2) + chip * piece[i] if i else me * piece[0]
        return pl.ds(pl.multiple_of(at, 8), piece[i])

    def first_copy(d):
        target = lax.rem(me + d, ways)
        return remote(
            acc.at[pl.ds(pl.multiple_of(target * piece[0], 8), piece[0])], first_got.at[d - 1],
            sum_send.at[0], sum_recv.at[0], place(me + d),
        )

    def core_copy(i):
        count = rows[i] // 2
        return remote(
            acc.at[pl.ds(pl.multiple_of(base[i] + (1 - core) * count, 8), count)],
            core_got.at[pl.ds(core_at[i], count)],
            core_send.at[i], core_recv.at[i], {"state": partner(1)},
        )

    def sum_copy(i, d):
        target = lax.rem(chip + d, chips)
        at = base[i] + core * (rows[i] // 2) + target * piece[i]
        return remote(
            acc.at[pl.ds(pl.multiple_of(at, 8), piece[i])],
            piece_got.at[d - 1, pl.ds(piece_at[i], piece[i])],
            sum_send.at[i], sum_recv.at[i], place(target * 2 + core),
        )

    def send_sums(i):
        for d in range(1, chips):
            sum_copy(i, d).start()

    def all_copies(i):
        if i < spread_rows:
            targets = [place(me + d) for d in range(1, ways)]
        else:
            targets = [place(lax.rem(chip + d, chips) * 2 + core) for d in range(1, chips)]
        return [
            remote(full.at[all_pieces(i)], full.at[all_pieces(i)], all_send.at[i], all_recv.at[i], to)
            for to in targets
        ]

    def pass_copy(i):
        count = rows[i] // 2
        ref = full.at[pl.ds(pl.multiple_of(base[i] + core * count, 8), count)]
        return remote(ref, ref, pass_send.at[i], pass_recv.at[i], {"state": partner(1)})

    def whole_first():
        return remote(first_got, first_got, sum_send.at[0], sum_recv.at[0], place(me + 1))

    def whole_sum(i):
        ref = piece_got.at[:, pl.ds(piece_at[i], piece[i])]
        return remote(ref, ref, sum_send.at[i], sum_recv.at[i], place(me + 1))

    def whole_all(i):
        count = (ways if i < spread_rows else chips) - 1
        ref = full.at[pl.ds(base[i], count * piece[i])]
        return remote(ref, ref, all_send.at[i], all_recv.at[i], place(me + 1))

    gram_row(0)
    for d in range(1, ways):
        first_copy(d).start()
    for i in range(1, blocks - 1):
        gram_row(i)
        core_copy(i).start()
    gram_row(blocks - 1)
    innovation = [inno[pl.ds(low + i, 1), :] for i in range(own)]
    innovation = split(jnp.broadcast_to(jnp.concatenate(innovation, axis=1), (16, own * BLK)))
    rhs = lax.dot_general(
        jnp.concatenate([innovation[0], innovation[0], innovation[1]], axis=1),
        jnp.concatenate([both[0], both[1], both[0]], axis=0),
        (((1,), (0,)), ((), ())), preferred_element_type=jnp.float32,
    )
    rhs_at = base[-1] + blocks * BLK
    for j in range(blocks):
        acc[rhs_at + j : rhs_at + j + 1, :] = rhs[0:1, j * BLK : (j + 1) * BLK]
    core_copy(blocks - 1).start()
    for i in range(1, blocks):
        core_copy(i).wait_recv()
        mine = pl.ds(pl.multiple_of(base[i] + core * (rows[i] // 2), 8), rows[i] // 2)
        acc[mine, :] += core_got[core_at[i] : core_at[i] + rows[i] // 2, :]
        if i == 1:
            send_sums(1)

    def gather_row(i):
        if i:
            whole_sum(i).wait_recv()
        else:
            whole_first().wait_recv()
        value = acc[all_pieces(i), :]
        for d in range(1, chips if i else ways):
            if i:
                value += piece_got[d - 1, piece_at[i] : piece_at[i] + piece[i], :]
            else:
                value += first_got[d - 1]
        full[all_pieces(i), :] = value
        for copy in all_copies(i):
            copy.start()

    row = lax.broadcasted_iota(jnp.int32, (BLK, BLK), 0)
    col = lax.broadcasted_iota(jnp.int32, (BLK, BLK), 1)
    ridge = jnp.where(row == col, members - 1.0, 0.0)

    def block_of(i, j):
        value = full[base[i] + j * BLK : base[i] + (j + 1) * BLK, :]
        return value + ridge if i == j else value

    ncells = slab.shape[1]
    inverse, factor, solved, solved_split = [], {}, [], []

    def reduced(value, parts, i):
        if not parts:
            return value
        x = [jnp.concatenate([p[n] for p in parts], axis=1) for n in range(2)]
        y = [jnp.concatenate([factor[i, m][n] for m in range(len(parts))], axis=1) for n in range(2)]
        return value - times_transposed(x, y)

    def solve(i):
        value = slab[me_o, :, i * BLK : (i + 1) * BLK].astype(jnp.float32)
        value = reduced(value, solved_split, i)
        solved.append(times_transposed(split(value), inverse[i]))
        solved_split.append(split(solved[i]))

    def pass_row(i):
        whole_all(i).wait_recv()
        pass_copy(i).start()

    due = {}

    def plan(step, row, at):
        if row < blocks:
            due.setdefault(at, []).append(functools.partial(step, row))

    plan(gather_row, 2, (0, 1))
    plan(pass_row, 1, (0, 2))
    plan(gather_row, 3, (0, 3))
    plan(pass_row, 2, (1, 1))
    plan(pass_row, 3, (2, 0))

    def during(i, panel):
        for step in due.get((i, panel), []):
            step()

    middle, middle_split = [], []

    def solve_middle(i):
        value = jnp.broadcast_to(full[rhs_at + i : rhs_at + i + 1, :], (16, BLK))
        value = reduced(value, middle_split, i)
        middle.append(times_transposed(split(value), inverse[i]))
        middle_split.append(split(middle[i]))

    send_sums(2)
    gather_row(0)
    gather_row(1)
    send_sums(3)
    whole_all(0).wait_recv()
    for i in range(blocks):
        if i:
            if i < spread_rows:
                whole_all(i).wait_recv()
            else:
                pass_copy(i).wait_recv()
            for k in range(i):
                value = reduced(block_of(i, k), [factor[i, m] for m in range(k)], k)
                factor[i, k] = split(times_transposed(split(value), inverse[k]))
        value = block_of(i, i)
        if i:
            value = reduced(value, [factor[i, m] for m in range(i)], i)
            solve(i - 1)
        if i == blocks - 1:
            for k in range(i):
                solve_middle(k)
        inverse.append(split(inverse_factor(value, between=functools.partial(during, i))))
    solve(blocks - 1)
    solve_middle(blocks - 1)
    shift = jnp.zeros((ncells, 1), jnp.float32)
    for i in range(blocks):
        shift += jnp.sum(solved[i] * middle[i][0:1], axis=1, keepdims=True)
    root = (members - 1.0) ** 0.5
    offset = jnp.broadcast_to(mean_row[...], (BLK, ncells)).T[:, 0:1] + shift
    for i in range(blocks):
        out_ref[:, i * BLK : (i + 1) * BLK] = (offset + root * solved[i]).astype(jnp.bfloat16)

    for slot, delta in enumerate(reach):
        @pl.when(inside(delta))
        def _():
            for h in range(2):
                slab_copy(me_o, slot, h, clip(me_o + delta)).wait_send()
    for slot, delta in enumerate(far):
        @pl.when(inside(delta))
        def _():
            mean_copy(me_o, slot, clip(me_o + delta)).wait_send()
    for at, block, to in relays:
        @pl.when(me_o == at)
        def _():
            for h in range(2):
                slab_copy(block, 4, h, to).wait_send()
    for t in range(len(state_bits)):
        for i in range(nb >> (t + 1)):
            part_copy(t, i).wait_send()
    whole_first().wait_send()
    whole_all(0).wait_send()
    for i in range(1, blocks):
        core_copy(i).wait_send()
        whole_sum(i).wait_send()
        whole_all(i).wait_send()
        if i >= spread_rows:
            pass_copy(i).wait_send()


def fused(obs_n, state_n, ids, counts, cells, mean_row, ops, readings, stds):
    nb = ops.shape[0]
    members = cells.shape[1]
    blocks = members // BLK
    ways = obs_n * state_n
    total = BLK * blocks * (blocks + 1) // 2 + BLK
    rounds = len(bits_of(state_n))
    dma = lambda *shape: pltpu.SemaphoreType.DMA(shape)
    return pl.pallas_call(
        functools.partial(fused_kernel, obs_n, state_n),
        out_shape=jax.ShapeDtypeStruct(cells.shape, jnp.bfloat16),
        in_specs=[pl.BlockSpec(memory_space=pltpu.SMEM)] * 2
        + [pl.BlockSpec(memory_space=pl.ANY)] * 5,
        out_specs=pl.BlockSpec(memory_space=pltpu.VMEM),
        scratch_shapes=[
            pltpu.VMEM(mean_row.shape, jnp.float32),
            pltpu.VMEM(ops.shape, jnp.bfloat16),
            pltpu.VMEM((nb, BLK), jnp.float32),
            pltpu.VMEM((nb, BLK), jnp.float32),
            dma(5),
            pltpu.VMEM((obs_n, BLK, members), jnp.bfloat16),
            pltpu.VMEM((obs_n, 16, BLK), jnp.bfloat16),
            pltpu.VMEM((obs_n, nb * BLK, 2 * BLK), jnp.bfloat16),
            pltpu.VMEM((nb * BLK, members), jnp.float32),
            pltpu.VMEM((nb // state_n, BLK, members), jnp.float32),
            pltpu.VMEM((nb, BLK, members), jnp.bfloat16),
            pltpu.VMEM((nb, BLK, members), jnp.bfloat16),
            pltpu.VMEM((nb, BLK), jnp.float32),
            pltpu.VMEM((rounds, nb, BLK), jnp.float32),
            pltpu.VMEM((total, BLK), jnp.float32),
            pltpu.VMEM(((total - BLK) // 2, BLK), jnp.float32),
            pltpu.VMEM((ways - 1, BLK // ways, BLK), jnp.float32),
            pltpu.VMEM((ways // 2 - 1, (total - BLK) // ways, BLK), jnp.float32),
            pltpu.VMEM((total, BLK), jnp.float32),
            dma(5, 2), dma(obs_n, 2), dma(6), dma(obs_n),
            dma(nb), dma(nb), dma(rounds), dma(rounds),
            dma(blocks), dma(blocks), dma(blocks), dma(blocks), dma(blocks), dma(blocks),
            dma(blocks), dma(blocks),
        ],
        compiler_params=pltpu.CompilerParams(
            collective_id=0, has_side_effects=True, vmem_limit_bytes=60 << 20
        ),
    )(ids, counts, cells, mean_row, ops, readings, stds)


def local(
    obs_n,
    state_n,
    anomalies,
    prior_ensemble_mean,
    operator_blocks,
    block_column_ids,
    observation_counts,
    observed_readings,
    observation_error_std,
):
    cells = anomalies[0]
    if obs_n == 4 and state_n == 4 and cells.shape[0] == BLK and 1 < cells.shape[1] // BLK <= 8:
        return fused(
            obs_n, state_n, block_column_ids[:, 0], observation_counts, cells, prior_ensemble_mean,
            operator_blocks[:, 0], observed_readings, observation_error_std,
        )[None]
    packed = observe(
        obs_n, state_n, block_column_ids[:, 0], observation_counts, cells, prior_ensemble_mean,
        operator_blocks[:, 0], observed_readings, observation_error_std,
    )
    return finish(packed, cells, prior_ensemble_mean)[None]


def solution(mesh):
    placed = (
        P("state", "obs", None),
        P("state", "obs"),
        P(("net", "obs"), "state", None, None, None),
        P(("net", "obs"), "state", None),
        P(("net", "obs")),
        P(("net", "obs"), None),
        P(("net", "obs"), None),
    )
    return jax.shard_map(
        functools.partial(local, mesh.shape["obs"], mesh.shape["state"]),
        mesh=mesh,
        in_specs=placed,
        out_specs=P(("net", "state"), "obs", None),
        check_vma=False,
    )
```

```python
import functools
import jax
import jax.numpy as jnp
from jax import lax
from jax.experimental import pallas as pl
from jax.experimental.pallas import tpu as pltpu
from jax.sharding import PartitionSpec as P

BLK = 128
HI = lax.Precision.HIGHEST
NT = (((1,), (1,)), ((), ()))


TN = (((0,), (0,)), ((), ()))


def split(x):
    high = x.astype(jnp.bfloat16)
    return high, (x - high.astype(jnp.float32)).astype(jnp.bfloat16)


def joined(x, y, axis, dims):
    (xh, xl), (yh, yl) = x, y
    return lax.dot_general(
        jnp.concatenate([xh, xh, xl], axis=axis), jnp.concatenate([yh, yl, yh], axis=axis), dims,
        preferred_element_type=jnp.float32,
    )


def times_transposed(x, y):
    return joined(x, y, 1, NT)


def transposed_times(x, y):
    return joined(x, y, 0, TN)


def inverse_factor(block, width=32, between=None):
    row = lax.broadcasted_iota(jnp.int32, (BLK, BLK), 0)
    col = lax.broadcasted_iota(jnp.int32, (BLK, BLK), 1)
    eye = (row == col).astype(jnp.float32)
    groups = BLK // 8
    left = [block[8 * g : 8 * g + 8] for g in range(groups)]
    right = [eye[8 * g : 8 * g + 8] for g in range(groups)]
    sub = lax.broadcasted_iota(jnp.int32, (8, 1), 0)
    lane = lax.broadcasted_iota(jnp.int32, (1, BLK), 1)
    local = width // 8
    for start in range(0, BLK, width):
        if between:
            between(start // width)
        g0 = start // 8
        spread = [
            [
                None if h < j // 8
                else jnp.broadcast_to(left[g0 + h][:, start + j : start + j + 1], (8, BLK))
                for h in range(local)
            ]
            for j in range(width)
        ]
        scaled = []
        roots = []
        for j in range(width):
            gj, ij = divmod(j, 8)
            pivot = spread[j][gj][ij : ij + 1]
            inv = 1.0 / pivot
            roots.append(lax.rsqrt(pivot))
            lrow = left[g0 + gj][ij : ij + 1]
            rrow = right[g0 + gj][ij : ij + 1]
            scaled.append(lrow * inv)
            ms = {}
            for h in range(gj, local):
                m = spread[j][h]
                if h == gj:
                    if ij == 7:
                        continue
                    m = jnp.where(sub > ij, m, 0.0)
                ms[h] = m * inv
            for t in range(j + 1, width):
                gt, it = divmod(t, 8)
                shared = spread[j][gt][it : it + 1]
                for h in range(gt, local):
                    if h in ms:
                        spread[t][h] = spread[t][h] - ms[h] * shared
            for h in ms:
                left[g0 + h] = left[g0 + h] - ms[h] * lrow
                right[g0 + h] = right[g0 + h] - ms[h] * rrow
        upper_l = jnp.concatenate(left[g0 : g0 + local], axis=0)
        upper_r = jnp.concatenate(right[g0 : g0 + local], axis=0)
        end = start + width
        if end < BLK:
            low = jnp.where(lane >= end, jnp.concatenate(scaled, axis=0), 0.0)
            change = transposed_times(
                split(low), split(jnp.concatenate([upper_l, upper_r], axis=1))
            )
            for h in range(end // 8, groups):
                left[h] = left[h] - change[8 * h : 8 * h + 8, :BLK]
                right[h] = right[h] - change[8 * h : 8 * h + 8, BLK:]
        scale = jnp.concatenate(roots, axis=0)
        for h in range(local):
            right[g0 + h] = right[g0 + h] * scale[8 * h : 8 * h + 8]
    return jnp.concatenate(right, axis=0)


def finish_kernel(packed_ref, anom_ref, mean_ref, out_ref, work):
    cells, members = anom_ref.shape
    total = members + cells + 8
    row = lax.broadcasted_iota(jnp.int32, (BLK, BLK), 0)
    col = lax.broadcasted_iota(jnp.int32, (BLK, BLK), 1)
    ridge = jnp.where(row == col, members - 1.0, 0.0)
    start = 0
    last = packed_ref.shape[0] - 8
    for j in range(members // BLK):
        size = members - j * BLK
        cols = slice(j * BLK, (j + 1) * BLK)
        if j:
            work[0 : j * BLK, cols] = jnp.zeros((j * BLK, BLK), jnp.float32)
        work[cols, cols] = packed_ref[start : start + BLK, :] + ridge
        if size > BLK:
            work[(j + 1) * BLK : members, cols] = packed_ref[start + BLK : start + size, :]
        start += size
    for j in range(members // BLK):
        cols = slice(j * BLK, (j + 1) * BLK)
        work[members + cells : total, cols] = jnp.broadcast_to(
            packed_ref[last + j : last + j + 1, :], (8, BLK)
        )
    work[members : members + cells, :] = anom_ref[...].astype(jnp.float32)

    for off in range(0, members, BLK):
        end = off + BLK
        inv = inverse_factor(work[off:end, off:end])
        x = lax.dot_general(
            work[end:total, off:end], inv, NT, precision=HI, preferred_element_type=jnp.float32
        )
        work[members:total, off:end] = x[members - end :]
        if end < members:
            work[end : end + BLK, end : end + BLK] -= lax.dot_general(
                x[:BLK], x[:BLK], NT, precision=HI, preferred_element_type=jnp.float32
            )
            work[end + BLK : total, end : end + BLK] -= lax.dot_general(
                x[BLK:], x[:BLK], NT, precision=HI, preferred_element_type=jnp.float32
            )
        for at in range(end + BLK, members, BLK):
            work[at:total, at : at + BLK] -= lax.dot_general(
                x[at - end :], x[at - end : at - end + BLK], NT, precision=HI,
                preferred_element_type=jnp.float32,
            )

    solved = work[members : members + cells, :]
    shift = jnp.sum(solved * work[members + cells : members + cells + 1, :], axis=1, keepdims=True)
    root = (members - 1.0) ** 0.5
    mean = jnp.broadcast_to(mean_ref[...], (BLK, cells)).T[:, 0:1]
    out_ref[...] = (mean + (root * solved + shift)).astype(jnp.bfloat16)


def finish(packed, cells, mean_row):
    ncells, members = cells.shape
    return pl.pallas_call(
        finish_kernel,
        out_shape=jax.ShapeDtypeStruct((ncells, members), jnp.bfloat16),
        in_specs=[pl.BlockSpec(memory_space=pltpu.VMEM)] * 3,
        out_specs=pl.BlockSpec(memory_space=pltpu.VMEM),
        scratch_shapes=[pltpu.VMEM((members + ncells + 8, members), jnp.float32)],
        compiler_params=pltpu.CompilerParams(vmem_limit_bytes=32 << 20),
    )(packed, cells, mean_row)


def packed_rows(members, ways):
    need = sum(members - j * BLK for j in range(members // BLK))
    step = 16 * ways
    return (need + step - 1) // step * step


def bits_of(n):
    return [1 << t for t in range(n.bit_length() - 1)]


def observe_kernel(
    obs_n, state_n, ids_ref, counts_ref, cells_hbm, mean_hbm, ops_hbm, read_hbm, std_hbm, out_ref,
    mean_row, ops_ref, read_ref, std_ref, load_sem,
    slab, slab_mean, part, sent, got, inno, inno_got, acc, acc_got, full, rhs_sum, rhs_got,
    right_send, right_recv, left_send, left_recv, part_send, part_recv, inno_send, inno_recv,
    acc_send, acc_recv, rhs_send, rhs_recv,
):
    me_o, me_s = lax.axis_index("obs"), lax.axis_index("state")
    nb, slots = ops_ref.shape[0], ops_ref.shape[1]
    members = slab.shape[2]
    state_bits, obs_bits = bits_of(state_n), bits_of(obs_n)

    loads = [
        pltpu.make_async_copy(src, dst, load_sem.at[n])
        for n, (src, dst) in enumerate([
            (cells_hbm, slab.at[me_o]), (mean_hbm, mean_row), (read_hbm, read_ref),
            (std_hbm, std_ref), (ops_hbm, ops_ref),
        ])
    ]
    for load in loads:
        load.start()

    def partner(axis, bit):
        me = me_s if axis == "state" else me_o
        return me + bit - 2 * bit * ((me // bit) % 2)

    barrier = pltpu.get_barrier_semaphore()
    greeted = [{"obs": lax.rem(me_o + 1, obs_n)}, {"obs": lax.rem(me_o + obs_n - 1, obs_n)}]
    greeted += [{"obs": partner("obs", b)} for b in obs_bits]
    greeted += [{"state": partner("state", b)} for b in state_bits]
    for where in greeted:
        pl.semaphore_signal(barrier, inc=1, device_id=where, device_id_type=pl.DeviceIdType.MESH)
    loads[0].wait()
    loads[1].wait()
    slab_mean[me_o] = jnp.broadcast_to(mean_row[...], (16, BLK)).astype(jnp.bfloat16)
    pl.semaphore_wait(barrier, len(greeted))

    def remote(src, dst, send, recv, where):
        return pltpu.make_async_remote_copy(
            src_ref=src, dst_ref=dst, send_sem=send, recv_sem=recv,
            device_id=where, device_id_type=pl.DeviceIdType.MESH,
        )

    def hop(block, sends, recvs, t, to):
        return [
            remote(slab.at[block], slab.at[block], sends.at[0, t], recvs.at[0, t], {"obs": to}),
            remote(slab_mean.at[block], slab_mean.at[block], sends.at[1, t], recvs.at[1, t], {"obs": to}),
        ]

    def clip(x):
        return jnp.clip(x, 0, obs_n - 1)

    for t in range(obs_n - 1):
        @pl.when((me_o < obs_n - 1) & (me_o - t >= 0))
        def _():
            for c in hop(clip(me_o - t), right_send, right_recv, t, clip(me_o + 1)):
                c.start()

        @pl.when((me_o > 0) & (me_o + t <= obs_n - 1))
        def _():
            for c in hop(clip(me_o + t), left_send, left_recv, t, clip(me_o - 1)):
                c.start()

        @pl.when(me_o - 1 - t >= 0)
        def _():
            for c in hop(clip(me_o - 1 - t), right_send, right_recv, t, clip(me_o - 1)):
                c.wait_recv()

        @pl.when(me_o + 1 + t <= obs_n - 1)
        def _():
            for c in hop(clip(me_o + 1 + t), left_send, left_recv, t, clip(me_o + 1)):
                c.wait_recv()

    for load in loads[2:]:
        load.wait()
    lane = lax.broadcasted_iota(jnp.int32, (1, BLK), 1)

    def weight_of(b):
        return jnp.where(lane < counts_ref[b], 1.0 / std_ref[pl.ds(b, 1), :], 0.0)

    @pl.loop(0, nb)
    def _(b):
        mean = jnp.zeros((16, BLK), jnp.float32)
        for j in range(slots):
            mean += lax.dot_general(
                slab_mean[ids_ref[b, j]], ops_ref[b, j], NT, preferred_element_type=jnp.float32
            )
        share = read_ref[pl.ds(b, 1), :] * (1.0 / state_n)
        inno[pl.ds(b, 1), :] = weight_of(b) * (share - mean[0:1])

    def inno_copy(t):
        where = {"state": partner("state", state_bits[t])}
        return remote(inno, inno_got.at[t], inno_send.at[t], inno_recv.at[t], where)

    inno_copy(0).start()

    def observe(b):
        rows = jnp.zeros((BLK, members), jnp.float32)
        for j in range(slots):
            rows += jnp.dot(ops_ref[b, j], slab[ids_ref[b, j]], preferred_element_type=jnp.float32)
        return rows * jnp.broadcast_to(weight_of(b), (BLK, BLK)).T[:, 0:1]

    def part_copy(t, i):
        n = nb - (nb >> t) + i
        where = {"state": partner("state", state_bits[t])}
        return remote(sent.at[n], got.at[n], part_send.at[n], part_recv.at[n], where)

    lows = [0]
    for t, bit in enumerate(state_bits):
        half = nb >> (t + 1)
        keep = (me_s // bit) % 2 * half
        give = lows[-1] + half - keep
        lows.append(lows[-1] + keep)

        def total(b, upto):
            value = observe(b)
            for u in range(upto):
                part_copy(u, b - lows[u + 1]).wait_recv()
                value += got[nb - (nb >> u) + b - lows[u + 1]].astype(jnp.float32)
            return value

        @pl.loop(0, half)
        def _(i):
            sent[nb - (nb >> t) + i] = total(give + i, t).astype(jnp.bfloat16)
            part_copy(t, i).start()

        inno_copy(t).wait()
        inno[...] += inno_got[t]
        if t + 1 < len(state_bits):
            inno_copy(t + 1).start()
    own = nb // state_n
    low = lows[-1]
    last = len(state_bits) - 1

    @pl.loop(0, own)
    def _(i):
        value = observe(low + i)
        for u in range(last):
            part_copy(u, low + i - lows[u + 1]).wait_recv()
            value += got[nb - (nb >> u) + low + i - lows[u + 1]].astype(jnp.float32)
        part[i] = value

    @pl.loop(0, own)
    def _(i):
        part_copy(last, i).wait_recv()
        part[i] += got[nb - (nb >> last) + i].astype(jnp.float32)

    scaled = part[...].reshape(own * BLK, members)
    row = 0
    for j in range(members // BLK):
        size = members - j * BLK
        acc[row : row + size, :] = lax.dot_general(
            scaled[:, j * BLK :], scaled[:, j * BLK : (j + 1) * BLK], (((0,), (0,)), ((), ())),
            precision=HI, preferred_element_type=jnp.float32,
        )
        row += size
    if row < acc.shape[0]:
        acc[row:, :] = jnp.zeros((acc.shape[0] - row, BLK), jnp.float32)
    rhs = jnp.zeros((8, members), jnp.float32)
    for i in range(own):
        rhs += jnp.dot(
            jnp.broadcast_to(inno[pl.ds(low + i, 1), :], (8, BLK)), scaled[i * BLK : (i + 1) * BLK],
            precision=HI, preferred_element_type=jnp.float32,
        )
    rhs_sum[...] = jnp.zeros((8, BLK), jnp.float32)
    for j in range(members // BLK):
        rhs_sum[j : j + 1, :] = rhs[0:1, j * BLK : (j + 1) * BLK]

    by_state = [("state", b) for b in state_bits]
    by_obs = [("obs", b) for b in obs_bits]
    orders = [by_state + by_obs, by_state[:1] + by_obs + by_state[1:]]
    steps = len(orders[0])
    size = acc.shape[0] // 2
    bases = [0, size]
    spots = [0, size]
    trail = []
    for n in range(steps):
        size //= 2
        copies = []
        for k in range(2):
            axis, bit = orders[k][n]
            keep = ((me_s if axis == "state" else me_o) // bit) % 2 * size
            where = {axis: partner(axis, bit)}
            give = pl.multiple_of(bases[k] + size - keep, 8)
            copies.append(remote(
                acc.at[pl.ds(give, size)], acc_got.at[pl.ds(spots[k], size)],
                acc_send.at[k, n], acc_recv.at[k, n], where,
            ))
            bases[k] = pl.multiple_of(bases[k] + keep, 8)
            trail.append((k, n, where, bases[k], size))
            if k == 0:
                copies.append(remote(rhs_sum, rhs_got.at[n], rhs_send.at[n], rhs_recv.at[n], where))
        for copy in copies:
            copy.start()
        for copy in copies:
            copy.wait()
        for k in range(2):
            acc[pl.ds(bases[k], size), :] += acc_got[spots[k] : spots[k] + size, :]
            spots[k] += size
        rhs_sum[...] += rhs_got[n]
    for k in range(2):
        full[pl.ds(bases[k], size), :] = acc[pl.ds(bases[k], size), :]
    for n in reversed(range(steps)):
        copies = [
            remote(
                full.at[pl.ds(base, size)], full.at[pl.ds(base, size)],
                acc_send.at[k, steps + n], acc_recv.at[k, steps + n], where,
            )
            for k, m, where, base, size in trail if m == n
        ]
        for copy in copies:
            copy.start()
        for copy in copies:
            copy.wait()

    for t in range(obs_n - 1):
        @pl.when((me_o < obs_n - 1) & (me_o - t >= 0))
        def _():
            for c in hop(clip(me_o - t), right_send, right_recv, t, clip(me_o + 1)):
                c.wait_send()

        @pl.when((me_o > 0) & (me_o + t <= obs_n - 1))
        def _():
            for c in hop(clip(me_o + t), left_send, left_recv, t, clip(me_o - 1)):
                c.wait_send()
    for t in range(len(state_bits)):
        for i in range(nb >> (t + 1)):
            part_copy(t, i).wait_send()
    out_ref[0 : full.shape[0], :] = full[...]
    out_ref[full.shape[0] :, :] = rhs_sum[...]


def observe(obs_n, state_n, ids, counts, cells, mean_row, ops, readings, stds):
    nb = ops.shape[0]
    members = cells.shape[1]
    rows = packed_rows(members, obs_n * state_n)
    rounds = len(bits_of(state_n))
    steps = len(bits_of(obs_n)) + rounds
    hops = pltpu.SemaphoreType.DMA((2, obs_n - 1))
    dma = lambda *shape: pltpu.SemaphoreType.DMA(shape)
    return pl.pallas_call(
        functools.partial(observe_kernel, obs_n, state_n),
        out_shape=jax.ShapeDtypeStruct((rows + 8, BLK), jnp.float32),
        in_specs=[pl.BlockSpec(memory_space=pltpu.SMEM)] * 2
        + [pl.BlockSpec(memory_space=pl.ANY)] * 5,
        out_specs=pl.BlockSpec(memory_space=pltpu.VMEM),
        scratch_shapes=[
            pltpu.VMEM(mean_row.shape, jnp.float32),
            pltpu.VMEM(ops.shape, jnp.bfloat16),
            pltpu.VMEM((nb, BLK), jnp.float32),
            pltpu.VMEM((nb, BLK), jnp.float32),
            dma(5),
            pltpu.VMEM((obs_n, BLK, members), jnp.bfloat16),
            pltpu.VMEM((obs_n, 16, BLK), jnp.bfloat16),
            pltpu.VMEM((nb // state_n, BLK, members), jnp.float32),
            pltpu.VMEM((nb, BLK, members), jnp.bfloat16),
            pltpu.VMEM((nb, BLK, members), jnp.bfloat16),
            pltpu.VMEM((nb, BLK), jnp.float32),
            pltpu.VMEM((rounds, nb, BLK), jnp.float32),
            pltpu.VMEM((rows, BLK), jnp.float32),
            pltpu.VMEM((rows, BLK), jnp.float32),
            pltpu.VMEM((rows, BLK), jnp.float32),
            pltpu.VMEM((8, BLK), jnp.float32),
            pltpu.VMEM((steps, 8, BLK), jnp.float32),
            hops, hops, hops, hops,
            dma(nb), dma(nb), dma(rounds), dma(rounds),
            dma(2, 2 * steps), dma(2, 2 * steps), dma(steps), dma(steps),
        ],
        compiler_params=pltpu.CompilerParams(
            collective_id=0, has_side_effects=True, vmem_limit_bytes=60 << 20
        ),
    )(ids, counts, cells, mean_row, ops, readings, stds)


MESH = pl.DeviceIdType.MESH


def fused_kernel(
    obs_n, state_n, ids_ref, counts_ref, cells_hbm, mean_hbm, ops_hbm, read_hbm, std_hbm, out_ref,
    mean_row, ops_ref, read_ref, std_ref, load_sem,
    slab, slab_mean, wide, seen, part, sent, got, inno, inno_got, acc, core_got, first_got,
    piece_got, full,
    slab_send, slab_recv, mean_send, mean_recv, part_send, part_recv, inno_send, inno_recv,
    core_send, core_recv, sum_send, sum_recv, all_send, all_recv, pass_send, pass_recv,
):
    me_o, me_s = lax.axis_index("obs"), lax.axis_index("state")
    nb, slots = ops_ref.shape[0], ops_ref.shape[1]
    members = slab.shape[2]
    blocks = members // BLK
    state_bits = bits_of(state_n)
    ways = obs_n * state_n
    chips = ways // 2
    me = me_o * state_n + me_s
    chip, core = me // 2, me % 2

    loads = [
        pltpu.make_async_copy(src, dst, load_sem.at[n])
        for n, (src, dst) in enumerate([
            (cells_hbm, slab.at[me_o]), (mean_hbm, mean_row), (read_hbm, read_ref),
            (std_hbm, std_ref), (ops_hbm, ops_ref),
        ])
    ]
    for load in loads:
        load.start()

    def place(index):
        index = lax.rem(index, ways)
        return {"obs": index // state_n, "state": lax.rem(index, state_n)}

    barrier = pltpu.get_barrier_semaphore()
    for d in range(1, ways):
        pl.semaphore_signal(barrier, inc=1, device_id=place(me + d), device_id_type=MESH)
    loads[0].wait()
    loads[1].wait()
    slab_mean[me_o] = jnp.broadcast_to(mean_row[...], (16, BLK)).astype(jnp.bfloat16)
    pl.semaphore_wait(barrier, ways - 1)

    def remote(src, dst, send, recv, where):
        return pltpu.make_async_remote_copy(
            src_ref=src, dst_ref=dst, send_sem=send, recv_sem=recv,
            device_id=where, device_id_type=MESH,
        )

    def clip(x):
        return jnp.clip(x, 0, obs_n - 1)

    half_rows = BLK // 2

    def slab_copy(block, slot, h, to):
        rows = pl.ds(h * half_rows, half_rows)
        return remote(
            slab.at[block, rows], slab.at[block, rows],
            slab_send.at[slot, h], slab_recv.at[block, h], {"obs": to},
        )

    def mean_copy(block, slot, to):
        return remote(
            slab_mean.at[block], slab_mean.at[block],
            mean_send.at[slot], mean_recv.at[block], {"obs": to},
        )

    reach = [2, -2, 1, -1]
    far = [3, -3] + reach

    def inside(delta):
        return (me_o + delta >= 0) & (me_o + delta <= obs_n - 1)

    for slot, delta in enumerate(far):
        @pl.when(inside(delta))
        def _():
            mean_copy(me_o, slot, clip(me_o + delta)).start()
    for slot, delta in enumerate(reach):
        @pl.when(inside(delta))
        def _():
            for h in range(2):
                slab_copy(me_o, slot, h, clip(me_o + delta)).start()
    relays = [(2, 0, 3), (1, 3, 0)]
    pad = acc.shape[0] - BLK
    acc[pad:, :] = jnp.zeros((BLK, BLK), jnp.float32)
    for load in loads[2:]:
        load.wait()
    lane = lax.broadcasted_iota(jnp.int32, (1, BLK), 1)

    def weight_of(b):
        return jnp.where(lane < counts_ref[b], 1.0 / std_ref[pl.ds(b, 1), :], 0.0)

    @pl.loop(0, nb)
    def _(b):
        weight = jnp.broadcast_to(weight_of(b), (BLK, BLK)).T
        at = pl.ds(pl.multiple_of(b * BLK, BLK), BLK)
        for half in range(2):
            some = slice(half * half_rows, (half + 1) * half_rows)
            columns = [jnp.zeros((half_rows, BLK), jnp.float32) for _ in range(obs_n)]
            for j in range(slots):
                block = ops_ref[b, j, some, :].astype(jnp.float32)
                for c in range(obs_n):
                    columns[c] += jnp.where(ids_ref[b, j] == c, block, 0.0)
            at = pl.ds(pl.multiple_of(b * BLK + half * half_rows, half_rows), half_rows)
            for c in range(obs_n):
                high, low = split(columns[c] * weight[some, :])
                wide[c, at, 0:BLK] = high
                wide[c, at, BLK : 2 * BLK] = low

    def observe(c, start, count, first):
        block = slab[c]
        at = pl.ds(start, count)
        for n in range(0, members, 2 * BLK):
            cut = slice(n, n + 2 * BLK)
            weights = block[:, cut]
            value = jnp.dot(
                wide[c, at, :], jnp.concatenate([weights, weights], axis=0),
                preferred_element_type=jnp.float32,
            )
            if first:
                seen[at, cut] = value
            else:
                seen[at, cut] += value

    observe(me_o, 0, nb * BLK, True)

    order = [(0, 1, 2, 3), (1, 0, 2, 3), (2, 3, 1, 0), (3, 2, 1, 0)]

    def met(k):
        return sum(jnp.where(me_o == o, order[o][k], 0) for o in range(obs_n))

    for at, block, to in relays:
        @pl.when(me_o == at)
        def _():
            for h in range(2):
                slab_copy(block, 4, h, to).wait_recv()
                slab_copy(block, 4, h, to).start()

    for block in range(obs_n):
        @pl.when(me_o != block)
        def _():
            mean_copy(block, 0, 0).wait_recv()

    @pl.loop(0, nb)
    def _(b):
        mean = jnp.zeros((16, BLK), jnp.float32)
        for j in range(slots):
            mean += lax.dot_general(
                slab_mean[ids_ref[b, j]], ops_ref[b, j], NT, preferred_element_type=jnp.float32
            )
        share = read_ref[pl.ds(b, 1), :] * (1.0 / state_n)
        inno[pl.ds(b, 1), :] = weight_of(b) * (share - mean[0:1])

    def partner(bit):
        return me_s + bit - 2 * bit * ((me_s // bit) % 2)

    def inno_copy(t):
        where = {"state": partner(state_bits[t])}
        return remote(inno, inno_got.at[t], inno_send.at[t], inno_recv.at[t], where)

    inno_copy(0).start()
    for n in range(1, obs_n - 1):
        for h in range(2):
            slab_copy(met(n), 0, h, 0).wait_recv()
        observe(met(n), 0, nb * BLK, False)
    relayed = me_o < 0
    for at, _, _ in relays:
        relayed = relayed | (me_o == at)

    @pl.when(jnp.logical_not(relayed))
    def _():
        for h in range(2):
            slab_copy(met(obs_n - 1), 0, h, 0).wait_recv()

    def rows_of(b):
        return seen[pl.ds(pl.multiple_of(b * BLK, BLK), BLK), :]

    def part_copy(t, i):
        n = nb - (nb >> t) + i
        where = {"state": partner(state_bits[t])}
        return remote(sent.at[n], got.at[n], part_send.at[n], part_recv.at[n], where)

    for t in range(len(state_bits) - 1):
        inno_copy(t).wait()
        inno[...] += inno_got[t]
        inno_copy(t + 1).start()
    half = nb // 2
    keep = core * half
    for start in (half - keep, keep):
        observe(met(obs_n - 1), pl.multiple_of(start * BLK, BLK), half * BLK, False)
        if start is not keep:
            ahead = (1 - (me_s // 2) % 2) * (half // 2)

            @pl.loop(0, half)
            def _(n):
                i = lax.rem(n + ahead, half)
                sent[i] = rows_of(half - keep + i).astype(jnp.bfloat16)
                part_copy(0, i).start()

    lows = [0, keep]
    for t in range(1, len(state_bits)):
        half = nb >> (t + 1)
        keep = (me_s // state_bits[t]) % 2 * half
        give = lows[-1] + half - keep
        lows.append(lows[-1] + keep)

        @pl.loop(0, half)
        def _(i):
            value = rows_of(give + i)
            for u in range(t):
                part_copy(u, give + i - lows[u + 1]).wait_recv()
                value += got[nb - (nb >> u) + give + i - lows[u + 1]].astype(jnp.float32)
            sent[nb - (nb >> t) + i] = value.astype(jnp.bfloat16)
            part_copy(t, i).start()

    own = nb // state_n
    low = lows[-1]
    last = len(state_bits) - 1

    @pl.loop(0, own)
    def _(i):
        value = rows_of(low + i)
        for u in range(last):
            part_copy(u, low + i - lows[u + 1]).wait_recv()
            value += got[nb - (nb >> u) + low + i - lows[u + 1]].astype(jnp.float32)
        part[i] = value

    @pl.loop(0, own)
    def _(i):
        part_copy(last, i).wait_recv()
        part[i] += got[nb - (nb >> last) + i].astype(jnp.float32)

    rows = [(i + 1) * BLK + (BLK if i == blocks - 1 else 0) for i in range(blocks)]
    spread_rows = 0
    base = [sum(rows[:i]) for i in range(blocks)]
    piece = [r // ways for r in rows]
    core_at = [(base[i] - base[1]) // 2 if i else 0 for i in range(blocks)]
    piece_at = [sum(piece[1:i]) for i in range(blocks)]
    scaled = part[...].reshape(own * BLK, members)
    both = split(scaled)

    def columns(i, count):
        return [x[:, i * BLK : (i + count) * BLK] for x in both]

    def gram_row(i):
        result = transposed_times(columns(i, 1), columns(0, i + 1))
        for j in range(i + 1):
            acc[base[i] + j * BLK : base[i] + (j + 1) * BLK, :] = result[:, j * BLK : (j + 1) * BLK]

    def all_pieces(i):
        at = base[i] + core * (rows[i] // 2) + chip * piece[i]
        return pl.ds(pl.multiple_of(at, 8), piece[i])

    def first_copy(d):
        target = lax.rem(me + d, ways)
        at = lax.rem(target, 2) * (rows[0] // 2) + target // 2 * piece[0]
        return remote(
            acc.at[pl.ds(pl.multiple_of(at, 8), piece[0])], first_got.at[d - 1],
            sum_send.at[0], sum_recv.at[0], place(me + d),
        )

    def core_copy(i):
        count = rows[i] // 2
        return remote(
            acc.at[pl.ds(pl.multiple_of(base[i] + (1 - core) * count, 8), count)],
            core_got.at[pl.ds(core_at[i], count)],
            core_send.at[i], core_recv.at[i], {"state": partner(1)},
        )

    def sum_copy(i, d):
        target = lax.rem(chip + d, chips)
        at = base[i] + core * (rows[i] // 2) + target * piece[i]
        return remote(
            acc.at[pl.ds(pl.multiple_of(at, 8), piece[i])],
            piece_got.at[d - 1, pl.ds(piece_at[i], piece[i])],
            sum_send.at[i], sum_recv.at[i], place(target * 2 + core),
        )

    def send_sums(i):
        for d in range(1, chips):
            sum_copy(i, d).start()

    def all_copies(i):
        if i < spread_rows:
            targets = [place(me + d) for d in range(1, ways)]
        else:
            targets = [place(lax.rem(chip + d, chips) * 2 + core) for d in range(1, chips)]
        return [
            remote(full.at[all_pieces(i)], full.at[all_pieces(i)], all_send.at[i], all_recv.at[i], to)
            for to in targets
        ]

    def pass_copy(i):
        count = rows[i] // 2
        ref = full.at[pl.ds(pl.multiple_of(base[i] + core * count, 8), count)]
        return remote(ref, ref, pass_send.at[i], pass_recv.at[i], {"state": partner(1)})

    def whole_first():
        return remote(first_got, first_got, sum_send.at[0], sum_recv.at[0], place(me + 1))

    def whole_sum(i):
        ref = piece_got.at[:, pl.ds(piece_at[i], piece[i])]
        return remote(ref, ref, sum_send.at[i], sum_recv.at[i], place(me + 1))

    def whole_all(i):
        count = (ways if i < spread_rows else chips) - 1
        ref = full.at[pl.ds(base[i], count * piece[i])]
        return remote(ref, ref, all_send.at[i], all_recv.at[i], place(me + 1))

    gram_row(0)
    for d in range(1, ways):
        first_copy(d).start()
    for i in range(1, blocks - 1):
        gram_row(i)
        core_copy(i).start()
    gram_row(blocks - 1)
    inno_copy(last).wait()
    inno[...] += inno_got[last]
    innovation = [inno[pl.ds(low + i, 1), :] for i in range(own)]
    innovation = split(jnp.broadcast_to(jnp.concatenate(innovation, axis=1), (16, own * BLK)))
    rhs = lax.dot_general(
        jnp.concatenate([innovation[0], innovation[0], innovation[1]], axis=1),
        jnp.concatenate([both[0], both[1], both[0]], axis=0),
        (((1,), (0,)), ((), ())), preferred_element_type=jnp.float32,
    )
    rhs_at = base[-1] + blocks * BLK
    for j in range(blocks):
        acc[rhs_at + j : rhs_at + j + 1, :] = rhs[0:1, j * BLK : (j + 1) * BLK]
    core_copy(blocks - 1).start()
    for i in range(1, blocks):
        core_copy(i).wait_recv()
        mine = pl.ds(pl.multiple_of(base[i] + core * (rows[i] // 2), 8), rows[i] // 2)
        acc[mine, :] += core_got[core_at[i] : core_at[i] + rows[i] // 2, :]
        if i == 1:
            send_sums(1)

    def gather_row(i):
        if i:
            whole_sum(i).wait_recv()
        else:
            whole_first().wait_recv()
        value = acc[all_pieces(i), :]
        for d in range(1, chips if i else ways):
            if i:
                value += piece_got[d - 1, piece_at[i] : piece_at[i] + piece[i], :]
            else:
                value += first_got[d - 1]
        full[all_pieces(i), :] = value
        for copy in all_copies(i):
            copy.start()

    row = lax.broadcasted_iota(jnp.int32, (BLK, BLK), 0)
    col = lax.broadcasted_iota(jnp.int32, (BLK, BLK), 1)
    ridge = jnp.where(row == col, members - 1.0, 0.0)

    def block_of(i, j):
        value = full[base[i] + j * BLK : base[i] + (j + 1) * BLK, :]
        return value + ridge if i == j else value

    ncells = slab.shape[1]
    inverse, factor, solved, solved_split = [], {}, [], []

    def reduced(value, parts, i):
        if not parts:
            return value
        x = [jnp.concatenate([p[n] for p in parts], axis=1) for n in range(2)]
        y = [jnp.concatenate([factor[i, m][n] for m in range(len(parts))], axis=1) for n in range(2)]
        return value - times_transposed(x, y)

    def solve(i):
        value = slab[me_o, :, i * BLK : (i + 1) * BLK].astype(jnp.float32)
        value = reduced(value, solved_split, i)
        solved.append(times_transposed(split(value), inverse[i]))
        solved_split.append(split(solved[i]))

    def pass_row(i):
        whole_all(i).wait_recv()
        pass_copy(i).start()

    due = {}

    def plan(step, row, at):
        if row < blocks:
            due.setdefault(at, []).append(functools.partial(step, row))

    plan(gather_row, 2, (0, 1))
    plan(pass_row, 1, (0, 2))
    plan(gather_row, 3, (0, 3))
    plan(pass_row, 2, (1, 0))
    plan(pass_row, 3, (1, 3))

    def during(i, panel):
        for step in due.get((i, panel), []):
            step()

    middle, middle_split = [], []

    def solve_middle(i):
        value = jnp.broadcast_to(full[rhs_at + i : rhs_at + i + 1, :], (16, BLK))
        value = reduced(value, middle_split, i)
        middle.append(times_transposed(split(value), inverse[i]))
        middle_split.append(split(middle[i]))

    send_sums(2)
    gather_row(0)
    gather_row(1)
    send_sums(3)
    whole_all(0).wait_recv()
    pass_copy(0).start()
    pass_copy(0).wait_recv()
    for i in range(blocks):
        if i:
            if i < spread_rows:
                whole_all(i).wait_recv()
            else:
                pass_copy(i).wait_recv()
            for k in range(i):
                value = reduced(block_of(i, k), [factor[i, m] for m in range(k)], k)
                factor[i, k] = split(times_transposed(split(value), inverse[k]))
        value = block_of(i, i)
        if i:
            value = reduced(value, [factor[i, m] for m in range(i)], i)
            solve(i - 1)
        if i == blocks - 1:
            for k in range(i):
                solve_middle(k)
        inverse.append(split(inverse_factor(value, between=functools.partial(during, i))))
    solve(blocks - 1)
    solve_middle(blocks - 1)
    shift = jnp.zeros((ncells, 1), jnp.float32)
    for i in range(blocks):
        shift += jnp.sum(solved[i] * middle[i][0:1], axis=1, keepdims=True)
    root = (members - 1.0) ** 0.5
    offset = jnp.broadcast_to(mean_row[...], (BLK, ncells)).T[:, 0:1] + shift
    for i in range(blocks):
        out_ref[:, i * BLK : (i + 1) * BLK] = (offset + root * solved[i]).astype(jnp.bfloat16)

    for slot, delta in enumerate(reach):
        @pl.when(inside(delta))
        def _():
            for h in range(2):
                slab_copy(me_o, slot, h, clip(me_o + delta)).wait_send()
    for slot, delta in enumerate(far):
        @pl.when(inside(delta))
        def _():
            mean_copy(me_o, slot, clip(me_o + delta)).wait_send()
    for at, block, to in relays:
        @pl.when(me_o == at)
        def _():
            for h in range(2):
                slab_copy(block, 4, h, to).wait_send()
    for t in range(len(state_bits)):
        for i in range(nb >> (t + 1)):
            part_copy(t, i).wait_send()
    whole_first().wait_send()
    whole_all(0).wait_send()
    pass_copy(0).wait_send()
    for i in range(1, blocks):
        core_copy(i).wait_send()
        whole_sum(i).wait_send()
        whole_all(i).wait_send()
        if i >= spread_rows:
            pass_copy(i).wait_send()


def fused(obs_n, state_n, ids, counts, cells, mean_row, ops, readings, stds):
    nb = ops.shape[0]
    members = cells.shape[1]
    blocks = members // BLK
    ways = obs_n * state_n
    total = BLK * blocks * (blocks + 1) // 2 + BLK
    rounds = len(bits_of(state_n))
    dma = lambda *shape: pltpu.SemaphoreType.DMA(shape)
    return pl.pallas_call(
        functools.partial(fused_kernel, obs_n, state_n),
        out_shape=jax.ShapeDtypeStruct(cells.shape, jnp.bfloat16),
        in_specs=[pl.BlockSpec(memory_space=pltpu.SMEM)] * 2
        + [pl.BlockSpec(memory_space=pl.ANY)] * 5,
        out_specs=pl.BlockSpec(memory_space=pltpu.VMEM),
        scratch_shapes=[
            pltpu.VMEM(mean_row.shape, jnp.float32),
            pltpu.VMEM(ops.shape, jnp.bfloat16),
            pltpu.VMEM((nb, BLK), jnp.float32),
            pltpu.VMEM((nb, BLK), jnp.float32),
            dma(5),
            pltpu.VMEM((obs_n, BLK, members), jnp.bfloat16),
            pltpu.VMEM((obs_n, 16, BLK), jnp.bfloat16),
            pltpu.VMEM((obs_n, nb * BLK, 2 * BLK), jnp.bfloat16),
            pltpu.VMEM((nb * BLK, members), jnp.float32),
            pltpu.VMEM((nb // state_n, BLK, members), jnp.float32),
            pltpu.VMEM((nb, BLK, members), jnp.bfloat16),
            pltpu.VMEM((nb, BLK, members), jnp.bfloat16),
            pltpu.VMEM((nb, BLK), jnp.float32),
            pltpu.VMEM((rounds, nb, BLK), jnp.float32),
            pltpu.VMEM((total, BLK), jnp.float32),
            pltpu.VMEM(((total - BLK) // 2, BLK), jnp.float32),
            pltpu.VMEM((ways - 1, BLK // ways, BLK), jnp.float32),
            pltpu.VMEM((ways // 2 - 1, (total - BLK) // ways, BLK), jnp.float32),
            pltpu.VMEM((total, BLK), jnp.float32),
            dma(5, 2), dma(obs_n, 2), dma(6), dma(obs_n),
            dma(nb), dma(nb), dma(rounds), dma(rounds),
            dma(blocks), dma(blocks), dma(blocks), dma(blocks), dma(blocks), dma(blocks),
            dma(blocks), dma(blocks),
        ],
        compiler_params=pltpu.CompilerParams(
            collective_id=0, has_side_effects=True, vmem_limit_bytes=60 << 20
        ),
    )(ids, counts, cells, mean_row, ops, readings, stds)


def local(
    obs_n,
    state_n,
    anomalies,
    prior_ensemble_mean,
    operator_blocks,
    block_column_ids,
    observation_counts,
    observed_readings,
    observation_error_std,
):
    cells = anomalies[0]
    if obs_n == 4 and state_n == 4 and cells.shape[0] == BLK and 1 < cells.shape[1] // BLK <= 8:
        return fused(
            obs_n, state_n, block_column_ids[:, 0], observation_counts, cells, prior_ensemble_mean,
            operator_blocks[:, 0], observed_readings, observation_error_std,
        )[None]
    packed = observe(
        obs_n, state_n, block_column_ids[:, 0], observation_counts, cells, prior_ensemble_mean,
        operator_blocks[:, 0], observed_readings, observation_error_std,
    )
    return finish(packed, cells, prior_ensemble_mean)[None]


def solution(mesh):
    placed = (
        P("state", "obs", None),
        P("state", "obs"),
        P(("net", "obs"), "state", None, None, None),
        P(("net", "obs"), "state", None),
        P(("net", "obs")),
        P(("net", "obs"), None),
        P(("net", "obs"), None),
    )
    return jax.shard_map(
        functools.partial(local, mesh.shape["obs"], mesh.shape["state"]),
        mesh=mesh,
        in_specs=placed,
        out_specs=P(("net", "state"), "obs", None),
        check_vma=False,
    )
```
